512 devices in a mesh: ctx: 64 (over y, z), tp: 8 (over x, core).
Axes of the slice: x: 4, y: 4, z: 16, core: 2. Of those that a mesh axis runs over, the one named last changes fastest.
Arguments:
- query_rows: bfloat16 [32768, 4096], P('ctx', 'tp'), may hold values from -6 to 6
- key_rows: bfloat16 [32768, 4096], P('ctx', 'tp'), may hold values from -0.52734375 to 0.52734375
- value_rows: bfloat16 [32768, 4096], P('ctx', 'tp'), may hold values from -6 to 6
- log_decay: float32 [32, 32768], P('tp', 'ctx'), may hold values from -1 to 0
- norm_gain: float32 [4096], P('tp'), may hold values from 0.25 to 1.75
- out_weight: bfloat16 [4096, 3072], P(None, 'tp'), may hold values from -0.09375 to 0.09375
Outputs:
- projected: bfloat16 [32768, 3072], P('ctx', 'tp')
The draws below stay inside these ranges and needn't reach their ends.
All inputs are finite; a program needn't handle non-finite values.
Results may differ from the reference program's by a relative error of at most 0.015.
Values may be sent and summed in bfloat16 or wider, within the bound.
A program may use at most 64 MiB of HBM per device.

```python
import math
import jax
import jax.numpy as jnp
from jax import lax

HEADS = 32
HEAD_DIM = 128
D_OUT = 3072
BLOCK = 128
TOKENS = 32768


def draw_log_decay(key, part):
    keys_all = jax.random.split(jax.random.fold_in(key, 11), 6)
    fast_share = 0.5
    fast_head = jax.random.uniform(keys_all[0], (HEADS, 1)) < fast_share
    fast_rate = jnp.exp(jax.random.uniform(keys_all[1], (HEADS, 1), jnp.float32, math.log(1.0 / 50.0), math.log(1.0 / 30.0)))
    slow_rate = jax.random.uniform(keys_all[2], (HEADS, 1), jnp.float32, 0.05, 0.3) * 2.3 / TOKENS
    rate = jnp.where(fast_head, fast_rate, slow_rate)
    rough = jnp.exp(jax.random.uniform(keys_all[3], (HEADS, TOKENS), jnp.float32, -0.7, 0.7))
    spots = jax.random.randint(keys_all[4], (4,), 0, TOKENS)
    struck = jnp.any(jnp.arange(TOKENS)[None, :] == spots[:, None], axis=0)
    losses = jnp.log(jax.random.uniform(keys_all[5], (HEADS, TOKENS), jnp.float32, 0.5, 0.8))
    return (-rate * rough + jnp.where(struck[None, :], losses, 0.0)).astype(jnp.float32)


def levels(own_key, shape, cuts, least, largest):
    factor_of = 1.0
    for dim, parts in cuts:
        heights = jax.random.uniform(jax.random.fold_in(jax.random.fold_in(own_key, 6), dim), (parts,), jnp.float32, least / len(cuts), largest / len(cuts))
        factor_of = factor_of * jnp.repeat(jnp.exp(heights), shape[dim] // parts).reshape((-1,) + (1,) * (len(shape) - 1 - dim))
    return factor_of


def gaussian(key, dims, spread, bound, shards=(), dtype=jnp.bfloat16):
    factor_of = levels(key, dims, shards, -0.22, 0.18) if shards else 1.0
    values = jax.random.normal(key, dims, jnp.float32) * spread * factor_of
    return jnp.minimum(jnp.maximum(values, -bound), bound).astype(dtype)


def setup_inputs(seed: int = 0) -> dict:
    streams_of = jax.random.split(jax.random.key(seed), 7)
    return {
        "query_rows": gaussian(streams_of[0], (TOKENS, HEADS * HEAD_DIM), 1.0, 6.0, ((0, 64), (1, 8))),
        "key_rows": gaussian(streams_of[1], (TOKENS, HEADS * HEAD_DIM), (HEAD_DIM ** -0.5), 0.52734375, ((0, 64), (1, 8))),
        "value_rows": gaussian(streams_of[2], (TOKENS, HEADS * HEAD_DIM), 1.0, 6.0, ((0, 64), (1, 8))),
        "log_decay": draw_log_decay(jax.random.fold_in(streams_of[6], 71), 0),
        "norm_gain": jnp.clip(1.0 + 0.15 * jax.random.normal(streams_of[4], (HEADS * HEAD_DIM,), jnp.float32), 0.25, 1.75),
        "out_weight": gaussian(streams_of[5], (HEADS * HEAD_DIM, D_OUT), (HEADS * HEAD_DIM) ** -0.5, 0.09375, ((1, 8),)),
    }


def reference(query_rows, key_rows, value_rows, log_decay, norm_gain, out_weight):
    blocks = TOKENS // BLOCK
    q_block = query_rows.reshape(blocks, BLOCK, HEADS, HEAD_DIM).transpose(0, 2, 1, 3)
    k_block = key_rows.reshape(blocks, BLOCK, HEADS, HEAD_DIM).transpose(0, 2, 1, 3)
    v_block = value_rows.reshape(blocks, BLOCK, HEADS, HEAD_DIM).transpose(0, 2, 1, 3)
    decays = log_decay.reshape(HEADS, blocks, BLOCK).transpose(1, 0, 2)
    causal = jnp.arange(BLOCK)[:, None] >= jnp.arange(BLOCK)[None, :]

    def block_step(current_state, inputs):
        q_part, k_part, v_part, d_part = inputs
        cum = jnp.cumsum(d_part, axis=-1)
        spread_log = cum[:, :, None] - cum[:, None, :]
        factor = jnp.where(causal, jnp.exp(jnp.where(causal, spread_log, 0.0)), 0.0)
        scores = jnp.einsum('hte,hse->hts', q_part.astype(jnp.float32), k_part.astype(jnp.float32))
        weights = (scores * factor).astype(jnp.bfloat16)
        inside_part = jnp.einsum('hts,hse->hte', weights.astype(jnp.float32), v_part.astype(jnp.float32))
        carried_part = jnp.exp(cum)[:, :, None] * jnp.einsum('hte,hef->htf', q_part.astype(jnp.float32), current_state, precision=lax.Precision.HIGHEST)
        to_end = jnp.exp(cum[:, -1:] - cum)
        k_scaled = k_part.astype(jnp.float32) * to_end[:, :, None]
        next_state = jnp.exp(cum[:, -1])[:, None, None] * current_state + jnp.einsum('hse,hsf->hef', k_scaled, v_part.astype(jnp.float32), precision=lax.Precision.HIGHEST)
        return (next_state, inside_part + carried_part)
    start_state = jnp.zeros((HEADS, HEAD_DIM, HEAD_DIM), jnp.float32)
    _, pieces = lax.scan(block_step, start_state, (q_block, k_block, v_block, decays))
    attention = pieces.transpose(0, 2, 1, 3).reshape(TOKENS, HEADS * HEAD_DIM)
    scale = lax.rsqrt(lax.optimization_barrier(jnp.mean(attention * attention, axis=-1, keepdims=True)) + 1e-06)
    normed = (attention * scale * norm_gain).astype(jnp.bfloat16)
    return jnp.dot(normed, out_weight, preferred_element_type=jnp.float32).astype(jnp.bfloat16)
```

```python
import functools

import jax
import jax.numpy as jnp
from jax import lax
from jax.experimental import pallas as pl
from jax.experimental.pallas import tpu as pltpu
from jax.sharding import PartitionSpec as P

HEADS = 32
HEAD_DIM = 128
MESH = pl.DeviceIdType.MESH
F32 = jnp.float32
BF16 = jnp.bfloat16
LANES = 128
NZ = 16
NY = 4
NX = 4
FAR_FIRST = (8, 7, 9, 6, 10, 5, 11, 4, 12, 3, 13, 2, 14, 1, 15)


def dot(a, b, contract):
    return lax.dot_general(a, b, (contract, ((), ())), preferred_element_type=F32)


def column(row):
    return jnp.transpose(jnp.broadcast_to(row, (LANES, LANES)))


def kernel(
    q_hbm, k_hbm, v_hbm, ld_ref, gain_ref, w_hbm, out_ref,
    q_ref, k_ref, v_ref, w_ref, cum_ref, col_ref, att_ref, acc_ref,
    s_send, s_recv, d_send, d_recv, p_ref, p_log, t_send, t_recv, e_send, e_recv,
    p_send, i_ref, a_ref, ssq_ref,
    load_sem, s_ssem, s_rsem, d_ssem, d_rsem, t_ssem, t_rsem, e_ssem, e_rsem,
    p_ssem, p_rsem, q_ssem, q_rsem, r_ssem, l_ssem, c_ssem, a_rsem,
):
    heads, length = ld_ref.shape
    tiles = length // LANES
    ctx = lax.axis_index("ctx")
    tp = lax.axis_index("tp")
    y, z = ctx // NZ, lax.rem(ctx, NZ)
    x, core = tp // 2, lax.rem(tp, 2)

    def tp_at(dx, other):
        cx = lax.rem(x + dx, NX)
        cc = 1 - core if other else core
        return cx * 2 + cc

    def z_peer(i):
        return y * NZ + lax.rem(z + i, NZ)

    def y_peer(i):
        return lax.rem(y + i, NY) * NZ + z

    loads = [
        pltpu.make_async_copy(src, dst, load_sem.at[n])
        for n, (src, dst) in enumerate(
            ((k_hbm, k_ref), (v_hbm, v_ref), (q_hbm, q_ref), (w_hbm, w_ref))
        )
    ]
    for copy in loads:
        copy.start()

    barrier = pltpu.get_barrier_semaphore()
    for i in FAR_FIRST:
        pl.semaphore_signal(barrier, inc=1, device_id={"ctx": z_peer(i)}, device_id_type=MESH)
    for i in (2, 1, 3):
        pl.semaphore_signal(barrier, inc=1, device_id={"ctx": y_peer(i)}, device_id_type=MESH)
    tp_peers = [tp_at(dx, other) for dx in range(NX) for other in (False, True)][1:]
    for peer in tp_peers:
        pl.semaphore_signal(barrier, inc=1, device_id={"tp": peer}, device_id_type=MESH)

    steps = jnp.concatenate(
        [ld_ref[:, b * LANES : (b + 1) * LANES] for b in range(tiles)]
        + ([] if heads * tiles % 8 == 0 else [jnp.zeros((8 - heads * tiles % 8, LANES), F32)]),
        axis=0,
    )
    lane = lax.broadcasted_iota(jnp.int32, steps.shape, 1)
    shift = 1
    while shift < LANES:
        steps = steps + jnp.where(lane >= shift, pltpu.roll(steps, shift, 1), 0.0)
        shift *= 2
    before = jnp.zeros((heads, LANES), F32)
    for b in range(tiles):
        part = steps[b * heads : (b + 1) * heads, :] + before
        cum_ref[b * heads : (b + 1) * heads, :] = part
        before = jnp.broadcast_to(part[:, LANES - 1 :], (heads, LANES))
    for h in range(heads):
        d_send[h] = before[h : h + 1, :]

    loads[0].wait()
    loads[1].wait()
    for h in range(heads):
        span = slice(h * LANES, (h + 1) * LANES)
        total = d_send[h]
        pieces = []
        for b in range(tiles):
            rows = slice(b * LANES, (b + 1) * LANES)
            col = column(cum_ref[b * heads + h : b * heads + h + 1, :])
            col_ref[h, rows, :] = col
            pieces.append((k_ref[rows, span].astype(F32) * jnp.exp(total - col)).astype(BF16))
        scaled = jnp.concatenate(pieces, axis=0)
        state = dot(scaled, v_ref[:, span], ((0,), (0,)))
        s_send[h * 4 : (h + 1) * 4] = state.astype(BF16).reshape(4, 32, LANES)

    pl.semaphore_wait(barrier, (NZ - 1) + (NY - 1) + len(tp_peers))

    def s_copy(i):
        owner = lax.rem(z + i, NZ)
        return pltpu.make_async_remote_copy(
            src_ref=s_send.at[owner], dst_ref=s_recv.at[z], send_sem=s_ssem.at[i],
            recv_sem=s_rsem.at[i], device_id={"ctx": z_peer(i)}, device_id_type=MESH,
        )

    def d_copy(i):
        owner = lax.rem(z + i, NZ)
        return pltpu.make_async_remote_copy(
            src_ref=d_send.at[owner // 4], dst_ref=d_recv.at[z], send_sem=d_ssem.at[i],
            recv_sem=d_rsem.at[i], device_id={"ctx": z_peer(i)}, device_id_type=MESH,
        )

    for i in FAR_FIRST:
        d_copy(i).start()
        s_copy(i).start()
    s_recv[z] = s_send[z]
    d_recv[z] = d_send[z // 4]

    loads[2].wait()
    below = lax.broadcasted_iota(jnp.int32, (LANES, LANES), 0) >= lax.broadcasted_iota(
        jnp.int32, (LANES, LANES), 1
    )

    def inner_tile(h, b):
        span = slice(h * LANES, (h + 1) * LANES)
        rows = slice(b * LANES, (b + 1) * LANES)
        width = (b + 1) * LANES
        scores = dot(q_ref[rows, span], k_ref[:width, span], ((1,), (1,)))
        col = col_ref[h, rows, :]
        weights = []
        for s in range(b + 1):
            gap = col - cum_ref[s * heads + h : s * heads + h + 1, :]
            if s == b:
                factor = jnp.where(below, jnp.exp(jnp.where(below, gap, 0.0)), 0.0)
            else:
                factor = jnp.exp(gap)
            weights.append((scores[:, s * LANES : (s + 1) * LANES] * factor).astype(BF16))
        weight = weights[0] if b == 0 else jnp.concatenate(weights, axis=1)
        att_ref[rows, span] = dot(weight, v_ref[:width, span], ((1,), (0,)))

    for b in range(tiles):
        for h in range(heads):
            inner_tile(h, b)

    for i in FAR_FIRST:
        d_copy(i).wait_recv()
        s_copy(i).wait_recv()

    def scan_step(n, carry):
        state, log = carry
        p_ref[n] = state
        p_log[n] = log
        decay = d_recv[n]
        return jnp.exp(decay) * state + s_recv[n].astype(F32), log + decay

    state, log = lax.fori_loop(
        0, NZ, scan_step, (jnp.zeros((32, LANES), F32), jnp.zeros((1, LANES), F32)), unroll=True
    )
    t_send[...] = state
    e_send[...] = log

    def t_copy(i):
        return pltpu.make_async_remote_copy(
            src_ref=t_send, dst_ref=t_recv.at[y], send_sem=t_ssem.at[i],
            recv_sem=t_rsem.at[i], device_id={"ctx": y_peer(i)}, device_id_type=MESH,
        )

    def e_copy(i):
        return pltpu.make_async_remote_copy(
            src_ref=e_send, dst_ref=e_recv.at[y], send_sem=e_ssem.at[i],
            recv_sem=e_rsem.at[i], device_id={"ctx": y_peer(i)}, device_id_type=MESH,
        )

    for i in (2, 1, 3):
        e_copy(i).start()
        t_copy(i).start()
    t_recv[y] = state
    e_recv[y] = log
    for i in (1, 3, 2):
        e_copy(i).wait_recv()
        t_copy(i).wait_recv()
    entering = jnp.zeros((32, LANES), F32)
    for n in range(NY - 1):
        entering = jnp.where(n < y, jnp.exp(e_recv[n]) * entering + t_recv[n], entering)

    def p_copy(i):
        return pltpu.make_async_remote_copy(
            src_ref=p_send.at[lax.rem(z + i, NZ)], dst_ref=i_ref.at[z], send_sem=p_ssem.at[i],
            recv_sem=p_rsem.at[i], device_id={"ctx": z_peer(i)}, device_id_type=MESH,
        )

    for n in range(NZ):
        p_send[n] = (p_ref[n] + jnp.exp(p_log[n]) * entering).astype(BF16)
    for i in FAR_FIRST:
        p_copy(i).start()
    i_ref[z] = p_send[z]
    for i in FAR_FIRST:
        p_copy(i).wait_recv()

    for b in range(tiles):
        rows = slice(b * LANES, (b + 1) * LANES)
        squares = jnp.zeros((LANES, LANES), F32)
        for h in range(heads):
            span = slice(h * LANES, (h + 1) * LANES)
            state = i_ref[h * 4 : (h + 1) * 4].reshape(LANES, LANES)
            carried = dot(q_ref[rows, span], state, ((1,), (0,))) * jnp.exp(col_ref[h, rows, :])
            value = att_ref[rows, span] + carried
            squares = squares + value * value
            a_ref[tp, rows, span] = (value * gain_ref[:, span]).astype(BF16)
        ssq_ref[tp, :, rows] = jnp.sum(jnp.transpose(squares), axis=0, keepdims=True)

    def a_copy(slot, part, peer, ssem):
        rows = pl.ds(part * LANES, LANES)
        return pltpu.make_async_remote_copy(
            src_ref=a_ref.at[slot, rows], dst_ref=a_ref.at[slot, rows], send_sem=ssem,
            recv_sem=a_rsem.at[slot, part], device_id={"tp": peer}, device_id_type=MESH,
        )

    right, left, partner = tp_at(1, False), tp_at(NX - 1, False), tp_at(0, True)
    opposite = tp_at(2, False)
    right2, left2, opposite2 = tp_at(1, True), tp_at(NX - 1, True), tp_at(2, True)

    def ssq_copy(n):
        return pltpu.make_async_remote_copy(
            src_ref=ssq_ref.at[tp], dst_ref=ssq_ref.at[tp], send_sem=q_ssem.at[n],
            recv_sem=q_rsem.at[n], device_id={"tp": tp ^ (n + 1)}, device_id_type=MESH,
        )

    def ssq_from(n):
        slot = tp ^ (n + 1)
        return pltpu.make_async_remote_copy(
            src_ref=ssq_ref.at[slot], dst_ref=ssq_ref.at[slot], send_sem=q_ssem.at[n],
            recv_sem=q_rsem.at[n], device_id={"tp": slot}, device_id_type=MESH,
        )

    sent = []

    def start(slot, part, peer, ssem):
        copy = a_copy(slot, part, peer, ssem)
        copy.start()
        sent.append(copy)

    for n in range(7):
        ssq_copy(n).start()
    for r, l in zip((0, 1, 2, 3), (2, 3, 0, 1)):
        start(tp, r, right, r_ssem.at[r])
        start(tp, l, left, l_ssem.at[l])
        start(tp, r, partner, c_ssem.at[0, r])

    loads[3].wait()

    def project(slot, first=False):
        depth = a_ref.shape[2]
        product = dot(a_ref[slot], w_ref[pl.ds(pl.multiple_of(slot * depth, depth), depth), :], ((1,), (0,)))
        if first:
            acc_ref[...] = product
        else:
            acc_ref[...] += product

    def arrive(slot, part):
        a_copy(slot, part, partner, c_ssem.at[0, part]).wait_recv()

    project(tp, first=True)
    for r in range(tiles):
        arrive(partner, r)
    project(partner)
    for r, l in zip((0, 1, 2, 3), (2, 3, 0, 1)):
        arrive(left, r)
        if r < 2:
            start(left, r, right, r_ssem.at[4 + r])
        start(left, r, partner, c_ssem.at[1, r])
        arrive(right, l)
        if l >= 2:
            start(right, l, left, l_ssem.at[4 + l - 2])
        start(right, l, partner, c_ssem.at[2, l])
    project(left)
    project(right)
    for slot in (left2, right2):
        for r in range(tiles):
            arrive(slot, r)
        project(slot)
    for n in range(7):
        ssq_from(n).wait_recv()
    squares = ssq_ref[0]
    for n in range(1, 8):
        squares = squares + ssq_ref[n]
    scale = lax.rsqrt(squares / (HEADS * HEAD_DIM) + 1e-06)
    for r in (0, 2, 1, 3):
        arrive(opposite, r)
        start(opposite, r, partner, c_ssem.at[3, r])
    project(opposite)
    for r in (0, 2, 1, 3):
        arrive(opposite2, r)
    project(opposite2)
    for b in range(tiles):
        rows = slice(b * LANES, (b + 1) * LANES)
        col = column(scale[:, rows])
        for c in range(out_ref.shape[1] // LANES):
            cols = slice(c * LANES, (c + 1) * LANES)
            out_ref[rows, cols] = (acc_ref[rows, cols] * col).astype(BF16)

    for i in FAR_FIRST:
        d_copy(i).wait_send()
        s_copy(i).wait_send()
        p_copy(i).wait_send()
    for i in (1, 2, 3):
        e_copy(i).wait_send()
        t_copy(i).wait_send()
    for n in range(7):
        ssq_copy(n).wait_send()
    for copy in sent:
        copy.wait_send()


def per_device(query_rows, key_rows, value_rows, log_decay, norm_gain, out_weight):
    length, features = query_rows.shape
    heads = log_decay.shape[0]
    depth, width = out_weight.shape
    hbm = pl.BlockSpec(memory_space=pl.ANY)
    vmem = pl.BlockSpec(memory_space=pltpu.VMEM)
    dma = pltpu.SemaphoreType.DMA
    return pl.pallas_call(
        kernel,
        out_shape=jax.ShapeDtypeStruct((length, width), BF16),
        in_specs=[hbm, hbm, hbm, vmem, vmem, hbm],
        out_specs=vmem,
        scratch_shapes=[
            pltpu.VMEM((length, features), BF16),
            pltpu.VMEM((length, features), BF16),
            pltpu.VMEM((length, features), BF16),
            pltpu.VMEM((depth, width), BF16),
            pltpu.VMEM((16, LANES), F32),
            pltpu.VMEM((heads, length, LANES), F32),
            pltpu.VMEM((length, features), F32),
            pltpu.VMEM((length, width), F32),
            pltpu.VMEM((NZ, 32, LANES), BF16),
            pltpu.VMEM((NZ, 32, LANES), BF16),
            pltpu.VMEM((heads, 1, LANES), F32),
            pltpu.VMEM((NZ, 1, LANES), F32),
            pltpu.VMEM((NZ, 32, LANES), F32),
            pltpu.VMEM((NZ, 1, LANES), F32),
            pltpu.VMEM((32, LANES), F32),
            pltpu.VMEM((NY, 32, LANES), F32),
            pltpu.VMEM((1, LANES), F32),
            pltpu.VMEM((NY, 1, LANES), F32),
            pltpu.VMEM((NZ, 32, LANES), BF16),
            pltpu.VMEM((NZ, 32, LANES), BF16),
            pltpu.VMEM((8, length, features), BF16),
            pltpu.VMEM((8, 1, length), F32),
            dma((4,)),
            dma((NZ,)), dma((NZ,)), dma((NZ,)), dma((NZ,)),
            dma((NY,)), dma((NY,)), dma((NY,)), dma((NY,)),
            dma((NZ,)), dma((NZ,)),
            dma((7,)), dma((7,)),
            dma((6,)), dma((6,)), dma((4, 4)), dma((8, 4)),
        ],
        compiler_params=pltpu.CompilerParams(
            collective_id=0, has_side_effects=True, vmem_limit_bytes=48 * 1024 * 1024
        ),
        name="attention_layer",
    )(query_rows, key_rows, value_rows, log_decay, norm_gain.reshape(1, features), out_weight)


def solution(mesh):
    in_specs = (
        P("ctx", "tp"),
        P("ctx", "tp"),
        P("ctx", "tp"),
        P("tp", "ctx"),
        P("tp"),
        P(None, "tp"),
    )
    return jax.shard_map(
        per_device, mesh=mesh, in_specs=in_specs, out_specs=P("ctx", "tp"), check_vma=False
    )
```

```python
import functools

import jax
import jax.numpy as jnp
from jax import lax
from jax.experimental import pallas as pl
from jax.experimental.pallas import tpu as pltpu
from jax.sharding import PartitionSpec as P

HEADS = 32
HEAD_DIM = 128
MESH = pl.DeviceIdType.MESH
F32 = jnp.float32
BF16 = jnp.bfloat16
LANES = 128
NZ = 16
NY = 4
NX = 4
EARLY = 320
FAR = (8, 7, 9, 6, 10, 5, 11)
NEAR = (4, 12, 3, 13, 2, 14, 1, 15)
FAR_FIRST = FAR + NEAR


def dot(a, b, contract):
    return lax.dot_general(a, b, (contract, ((), ())), preferred_element_type=F32)


def column(row):
    return jnp.transpose(jnp.broadcast_to(row, (LANES, LANES)))


def kernel(
    q_hbm, k_hbm, v_hbm, ld_hbm, gain_hbm, w_hbm, out_ref,
    ld_ref, gain_ref, q_ref, k_ref, v_ref, w_ref, cum_ref, col_ref, att_ref, acc_ref,
    s_send, s_recv, d_send, d_recv, sf_ref, df_ref, p_ref, t_send, t_recv, e_send, e_recv,
    p_send, i_ref, qt_ref, al_ref, g_ref, a_ref, own_ref, sq_ref, ssq_ref,
    load_sem, s_ssem, s_rsem, d_ssem, d_rsem, sf_ssem, sf_rsem, df_ssem, df_rsem, t_ssem, t_rsem, e_ssem, e_rsem,
    p_ssem, p_rsem, q_ssem, q_rsem, x_ssem, x_rsem,
):
    heads, length = ld_ref.shape
    tiles = length // LANES
    ctx = lax.axis_index("ctx")
    tp = lax.axis_index("tp")
    y, z = ctx // NZ, lax.rem(ctx, NZ)
    x, core = tp // 2, lax.rem(tp, 2)

    def tp_at(dx, other):
        cx = lax.rem(x + dx, NX)
        cc = 1 - core if other else core
        return cx * 2 + cc

    def z_peer(i):
        return y * NZ + lax.rem(z + i, NZ)

    def y_peer(i):
        return lax.rem(y + i, NY) * NZ + z

    barrier = pltpu.get_barrier_semaphore()
    for i in NEAR:
        pl.semaphore_signal(barrier, inc=1, device_id={"ctx": z_peer(i)}, device_id_type=MESH)
    for i in (2, 1, 3):
        pl.semaphore_signal(barrier, inc=1, device_id={"ctx": y_peer(i)}, device_id_type=MESH)
    tp_peers = [tp_at(dx, other) for dx in range(NX) for other in (False, True)][1:]
    for peer in tp_peers:
        pl.semaphore_signal(barrier, inc=1, device_id={"tp": peer}, device_id_type=MESH)

    loads = [
        pltpu.make_async_copy(src, dst, load_sem.at[n])
        for n, (src, dst) in enumerate(
            (
                (k_hbm, k_ref), (v_hbm, v_ref), (q_hbm, q_ref), (w_hbm, w_ref),
                (ld_hbm, ld_ref), (gain_hbm, gain_ref),
            )
        )
    ]
    for n in (4, 0, 1, 2, 5):
        loads[n].start()
    waiting = [4, 0, 1, 2, 5]
    sent = []

    def need(n):
        loads[n].wait()
        waiting.remove(n)

    def go(copy):
        copy.start()
        sent.append(copy)

    need(4)
    steps = jnp.concatenate(
        [ld_ref[:, b * LANES : (b + 1) * LANES] for b in range(tiles)]
        + ([] if heads * tiles % 8 == 0 else [jnp.zeros((8 - heads * tiles % 8, LANES), F32)]),
        axis=0,
    )
    lane = lax.broadcasted_iota(jnp.int32, steps.shape, 1)
    shift = 1
    while shift < LANES:
        steps = steps + jnp.where(lane >= shift, pltpu.roll(steps, shift, 1), 0.0)
        shift *= 2
    before = jnp.zeros((heads, LANES), F32)
    for b in range(tiles):
        part = steps[b * heads : (b + 1) * heads, :] + before
        cum_ref[b * heads : (b + 1) * heads, :] = part
        before = jnp.broadcast_to(part[:, LANES - 1 :], (heads, LANES))
    for h in range(heads):
        d_send[h] = before[h : h + 1, :]

    need(0)
    need(1)
    for h in range(heads):
        span = slice(h * LANES, (h + 1) * LANES)
        total = d_send[h]
        pieces = []
        for b in range(tiles):
            rows = slice(b * LANES, (b + 1) * LANES)
            col = column(cum_ref[b * heads + h : b * heads + h + 1, :])
            col_ref[h, rows, :] = col
            pieces.append((k_ref[rows, span].astype(F32) * jnp.exp(total - col)).astype(BF16))
        scaled = jnp.concatenate(pieces, axis=0)
        state = dot(scaled, v_ref[:, span], ((0,), (0,)))
        s_send[h * 4 : (h + 1) * 4] = state.astype(BF16).reshape(4, 32, LANES)

    need(2)
    for h in range(heads):
        span = slice(h * LANES, (h + 1) * LANES)
        growth = jnp.exp(col_ref[h, :EARLY, :])
        qt_ref[tp, :, span] = (q_ref[:EARLY, span].astype(F32) * growth).astype(BF16)

    pl.semaphore_wait(barrier, len(NEAR) + (NY - 1) + len(tp_peers))

    def s_copy(i):
        owner = lax.rem(z + i, NZ)
        return pltpu.make_async_remote_copy(
            src_ref=s_send.at[owner], dst_ref=s_recv.at[z], send_sem=s_ssem.at[i],
            recv_sem=s_rsem.at[i], device_id={"ctx": z_peer(i)}, device_id_type=MESH,
        )

    def d_copy(i):
        owner = lax.rem(z + i, NZ)
        return pltpu.make_async_remote_copy(
            src_ref=d_send.at[owner // 4], dst_ref=d_recv.at[z], send_sem=d_ssem.at[i],
            recv_sem=d_rsem.at[i], device_id={"ctx": z_peer(i)}, device_id_type=MESH,
        )

    def via(i):
        return 4 if i <= 8 else NZ - 4

    def s_out(i):
        return pltpu.make_async_remote_copy(
            src_ref=s_send.at[lax.rem(z + i, NZ)], dst_ref=sf_ref.at[i - 5],
            send_sem=s_ssem.at[i], recv_sem=sf_rsem.at[i - 5],
            device_id={"ctx": z_peer(via(i))}, device_id_type=MESH,
        )

    def d_out(i):
        return pltpu.make_async_remote_copy(
            src_ref=d_send.at[lax.rem(z + i, NZ) // 4], dst_ref=df_ref.at[i - 5],
            send_sem=d_ssem.at[i], recv_sem=df_rsem.at[i - 5],
            device_id={"ctx": z_peer(via(i))}, device_id_type=MESH,
        )

    def s_on(i):
        return pltpu.make_async_remote_copy(
            src_ref=sf_ref.at[i - 5], dst_ref=s_recv.at[lax.rem(z + NZ - via(i), NZ)],
            send_sem=sf_ssem.at[i - 5], recv_sem=s_rsem.at[i],
            device_id={"ctx": z_peer(NZ - via(i) + i)}, device_id_type=MESH,
        )

    def d_on(i):
        return pltpu.make_async_remote_copy(
            src_ref=df_ref.at[i - 5], dst_ref=d_recv.at[lax.rem(z + NZ - via(i), NZ)],
            send_sem=df_ssem.at[i - 5], recv_sem=d_rsem.at[i],
            device_id={"ctx": z_peer(NZ - via(i) + i)}, device_id_type=MESH,
        )

    for i in FAR:
        go(d_out(i))
        go(s_out(i))
    for i in NEAR:
        go(d_copy(i))
        go(s_copy(i))
    loads[3].start()
    waiting.append(3)
    s_recv[z] = s_send[z]
    d_recv[z] = d_send[z // 4]

    right, left, partner = tp_at(1, False), tp_at(NX - 1, False), tp_at(0, True)
    opposite = tp_at(2, False)
    right2, left2, opposite2 = tp_at(1, True), tp_at(NX - 1, True), tp_at(2, True)

    class Flow:
        def __init__(self, kind, ref):
            self.kind, self.ref, self.half, self.count = kind, ref, ref.shape[1] // 2, 0

        def copy(self, slot, part, peer, number):
            view = self.ref.at[slot, pl.ds(part * self.half, self.half)]
            return pltpu.make_async_remote_copy(
                src_ref=view, dst_ref=view, send_sem=x_ssem.at[self.kind, number],
                recv_sem=x_rsem.at[self.kind, slot, part], device_id={"tp": peer},
                device_id_type=MESH,
            )

        def start(self, slot, part, peer):
            go(self.copy(slot, part, peer, self.count))
            self.count += 1

        def arrive(self, slot, part):
            self.copy(slot, part, partner, 0).wait_recv()

        def own(self):
            for r, l in ((0, 1), (1, 0)):
                self.start(tp, r, right)
                self.start(tp, l, left)
            for part in (0, 1):
                self.start(tp, part, partner)

        def first(self):
            self.arrive(left, 0)
            self.start(left, 0, right)
            self.start(left, 0, partner)
            self.arrive(right, 1)
            self.start(right, 1, left)
            self.start(right, 1, partner)

        def second(self):
            self.arrive(left, 1)
            self.start(left, 1, partner)
            self.arrive(right, 0)
            self.start(right, 0, partner)

        def last(self):
            for part in (0, 1):
                self.arrive(opposite, part)
                self.start(opposite, part, partner)

        def near(self, slot):
            for part in (0, 1):
                self.arrive(slot, part)

    q_flow, al_flow, g_flow, a_flow = (
        Flow(n, ref) for n, ref in enumerate((qt_ref, al_ref, g_ref, a_ref))
    )
    q_flow.own()

    below = lax.broadcasted_iota(jnp.int32, (LANES, LANES), 0) >= lax.broadcasted_iota(
        jnp.int32, (LANES, LANES), 1
    )

    def inner_tile(h, b):
        span = slice(h * LANES, (h + 1) * LANES)
        rows = slice(b * LANES, (b + 1) * LANES)
        width = (b + 1) * LANES
        scores = dot(q_ref[rows, span], k_ref[:width, span], ((1,), (1,)))
        col = col_ref[h, rows, :]
        weights = []
        for s in range(b + 1):
            gap = col - cum_ref[s * heads + h : s * heads + h + 1, :]
            if s == b:
                factor = jnp.where(below, jnp.exp(jnp.where(below, gap, 0.0)), 0.0)
            else:
                factor = jnp.exp(gap)
            weights.append((scores[:, s * LANES : (s + 1) * LANES] * factor).astype(BF16))
        weight = weights[0] if b == 0 else jnp.concatenate(weights, axis=1)
        att_ref[rows, span] = dot(weight, v_ref[:width, span], ((1,), (0,)))

    for b in range(tiles):
        for h in range(heads):
            inner_tile(h, b)
    need(5)
    al_ref[tp] = (att_ref[:EARLY, :] * gain_ref[...]).astype(BF16)
    al_flow.own()

    for i in FAR:
        d_out(i).wait_recv()
        go(d_on(i))
        s_out(i).wait_recv()
        go(s_on(i))

    for i in FAR_FIRST:
        d_copy(i).wait_recv()
    log = jnp.zeros((1, LANES), F32)
    reach, decays = [], []
    for n in range(NZ):
        reach.append(jnp.exp(log))
        decays.append(jnp.exp(d_recv[n]))
        log = log + d_recv[n]
    e_send[...] = log

    def t_copy(i):
        return pltpu.make_async_remote_copy(
            src_ref=t_send, dst_ref=t_recv.at[y], send_sem=t_ssem.at[i],
            recv_sem=t_rsem.at[i], device_id={"ctx": y_peer(i)}, device_id_type=MESH,
        )

    def e_copy(i):
        return pltpu.make_async_remote_copy(
            src_ref=e_send, dst_ref=e_recv.at[y], send_sem=e_ssem.at[i],
            recv_sem=e_rsem.at[i], device_id={"ctx": y_peer(i)}, device_id_type=MESH,
        )

    for i in (2, 1, 3):
        go(e_copy(i))
    e_recv[y] = log
    for i in FAR_FIRST:
        s_copy(i).wait_recv()
    state = jnp.zeros((32, LANES), F32)
    prefixes = []
    for n in range(NZ):
        prefixes.append(state)
        state = decays[n] * state + s_recv[n].astype(F32)
    t_send[...] = state
    for i in (2, 1, 3):
        go(t_copy(i))
    t_recv[y] = state
    for n in range(NZ):
        p_ref[n] = prefixes[n]
    q_flow.first()
    for i in (1, 3, 2):
        e_copy(i).wait_recv()
    row_decays = [jnp.exp(e_recv[n]) for n in range(NY - 1)]
    for i in (1, 3, 2):
        t_copy(i).wait_recv()
    entering = jnp.zeros((32, LANES), F32)
    for n in range(NY - 1):
        entering = jnp.where(n < y, row_decays[n] * entering + t_recv[n], entering)

    def p_copy(i):
        return pltpu.make_async_remote_copy(
            src_ref=p_send.at[lax.rem(z + i, NZ)], dst_ref=i_ref.at[z], send_sem=p_ssem.at[i],
            recv_sem=p_rsem.at[i], device_id={"ctx": z_peer(i)}, device_id_type=MESH,
        )

    for n in range(NZ):
        p_send[n] = (p_ref[n] + reach[n] * entering).astype(BF16)
    for i in FAR_FIRST:
        go(p_copy(i))
    i_ref[z] = p_send[z]

    depth, width = a_ref.shape[2], out_ref.shape[1]
    early, late = slice(0, EARLY), slice(EARLY, length)

    def weight_of(slot):
        return w_ref[pl.ds(pl.multiple_of(slot * depth, depth), depth), :]

    def add(rows, block, slot):
        acc_ref[rows, :] += dot(block, weight_of(slot), ((1,), (0,)))

    def add_inner(slot):
        add(early, al_ref[slot], slot)

    def add_carried(slot):
        parts = []
        for h in range(heads):
            span = slice(h * LANES, (h + 1) * LANES)
            parts.append(
                dot(qt_ref[slot, :, span], g_ref[slot, span, :], ((1,), (0,))).astype(BF16)
            )
        add(early, jnp.concatenate(parts, axis=1), slot)

    def add_late(slot):
        add(late, a_ref[slot], slot)

    q_flow.second()
    acc_ref[...] = jnp.zeros_like(acc_ref)
    need(3)
    q_flow.near(partner)
    al_flow.near(partner)
    add_inner(partner)
    al_flow.first()
    al_flow.second()
    add_inner(left)
    add_inner(right)
    for slot in (left2, right2):
        q_flow.near(slot)
        al_flow.near(slot)
        add_inner(slot)
    q_flow.last()

    for i in FAR_FIRST:
        p_copy(i).wait_recv()
    for h in range(heads):
        span = slice(h * LANES, (h + 1) * LANES)
        state = i_ref[h * 4 : (h + 1) * 4].reshape(LANES, LANES).astype(F32)
        g_ref[tp, span, :] = (state * gain_ref[:, span]).astype(BF16)
    g_flow.own()

    def finish(rows, store):
        squares = None
        for h in range(heads):
            span = slice(h * LANES, (h + 1) * LANES)
            state = i_ref[h * 4 : (h + 1) * 4].reshape(LANES, LANES)
            carried = dot(q_ref[rows, span], state, ((1,), (0,))) * jnp.exp(col_ref[h, rows, :])
            value = att_ref[rows, span] + carried
            squares = value * value if squares is None else squares + value * value
            store(span, (value * gain_ref[:, span]).astype(BF16))
        sq_ref[rows, :] = squares

    def store_late(span, value):
        a_ref[tp, :, span] = value

    def store_own(span, value):
        own_ref[:, span] = value

    finish(late, store_late)
    a_flow.own()
    finish(early, store_own)
    for b in range(tiles):
        rows = slice(b * LANES, (b + 1) * LANES)
        ssq_ref[tp, :, rows] = jnp.sum(jnp.transpose(sq_ref[rows, :]), axis=0, keepdims=True)

    def ssq_copy(n):
        return pltpu.make_async_remote_copy(
            src_ref=ssq_ref.at[tp], dst_ref=ssq_ref.at[tp], send_sem=q_ssem.at[n],
            recv_sem=q_rsem.at[n], device_id={"tp": tp ^ (n + 1)}, device_id_type=MESH,
        )

    def ssq_from(n):
        slot = tp ^ (n + 1)
        return pltpu.make_async_remote_copy(
            src_ref=ssq_ref.at[slot], dst_ref=ssq_ref.at[slot], send_sem=q_ssem.at[n],
            recv_sem=q_rsem.at[n], device_id={"tp": slot}, device_id_type=MESH,
        )

    for n in range(7):
        go(ssq_copy(n))
    add(early, own_ref[...], tp)
    add_late(tp)
    g_flow.near(partner)
    add_carried(partner)
    al_flow.last()
    g_flow.first()
    g_flow.second()
    a_flow.near(partner)
    add_late(partner)
    add_carried(left)
    add_carried(right)
    a_flow.first()
    a_flow.second()
    add_late(left)
    add_late(right)
    g_flow.last()
    add_inner(opposite)
    add_carried(opposite)
    for slot in (left2, right2, opposite2):
        if slot is opposite2:
            q_flow.near(slot)
            al_flow.near(slot)
            add_inner(slot)
        g_flow.near(slot)
        add_carried(slot)
        if slot is not opposite2:
            a_flow.near(slot)
            add_late(slot)
    for n in range(7):
        ssq_from(n).wait_recv()
    squares = ssq_ref[0]
    for n in range(1, 8):
        squares = squares + ssq_ref[n]
    scale = lax.rsqrt(squares / (HEADS * HEAD_DIM) + 1e-06)
    a_flow.last()
    add_late(opposite)
    a_flow.near(opposite2)
    add_late(opposite2)
    for b in range(tiles):
        rows = slice(b * LANES, (b + 1) * LANES)
        out_ref[rows, :] = (acc_ref[rows, :] * jnp.tile(column(scale[:, rows]), (1, width // LANES))).astype(BF16)

    for n in waiting:
        loads[n].wait()
    for copy in sent:
        copy.wait_send()


def per_device(query_rows, key_rows, value_rows, log_decay, norm_gain, out_weight):
    length, features = query_rows.shape
    heads = log_decay.shape[0]
    depth, width = out_weight.shape
    hbm = pl.BlockSpec(memory_space=pltpu.HBM)
    vmem = pl.BlockSpec(memory_space=pltpu.VMEM)
    dma = pltpu.SemaphoreType.DMA
    return pl.pallas_call(
        kernel,
        out_shape=jax.ShapeDtypeStruct((length, width), BF16),
        in_specs=[hbm] * 6,
        out_specs=vmem,
        scratch_shapes=[
            pltpu.VMEM((heads, length), F32),
            pltpu.VMEM((1, features), F32),
            pltpu.VMEM((length, features), BF16),
            pltpu.VMEM((length, features), BF16),
            pltpu.VMEM((length, features), BF16),
            pltpu.VMEM((depth, width), BF16),
            pltpu.VMEM((16, LANES), F32),
            pltpu.VMEM((heads, length, LANES), F32),
            pltpu.VMEM((length, features), F32),
            pltpu.VMEM((length, width), F32),
            pltpu.VMEM((NZ, 32, LANES), BF16),
            pltpu.VMEM((NZ, 32, LANES), BF16),
            pltpu.VMEM((heads, 1, LANES), F32),
            pltpu.VMEM((NZ, 1, LANES), F32),
            pltpu.VMEM((7, 32, LANES), BF16),
            pltpu.VMEM((7, 1, LANES), F32),
            pltpu.VMEM((NZ, 32, LANES), F32),
            pltpu.VMEM((32, LANES), F32),
            pltpu.VMEM((NY, 32, LANES), F32),
            pltpu.VMEM((1, LANES), F32),
            pltpu.VMEM((NY, 1, LANES), F32),
            pltpu.VMEM((NZ, 32, LANES), BF16),
            pltpu.VMEM((NZ, 32, LANES), BF16),
            pltpu.VMEM((8, EARLY, features), BF16),
            pltpu.VMEM((8, EARLY, features), BF16),
            pltpu.VMEM((8, features, LANES), BF16),
            pltpu.VMEM((8, length - EARLY, features), BF16),
            pltpu.VMEM((EARLY, features), BF16),
            pltpu.VMEM((length, LANES), F32),
            pltpu.VMEM((8, 1, length), F32),
            dma((6,)),
            dma((NZ,)), dma((NZ,)), dma((NZ,)), dma((NZ,)),
            dma((7,)), dma((7,)), dma((7,)), dma((7,)),
            dma((NY,)), dma((NY,)), dma((NY,)), dma((NY,)),
            dma((NZ,)), dma((NZ,)),
            dma((7,)), dma((7,)),
            dma((4, 14)), dma((4, 8, 2)),
        ],
        compiler_params=pltpu.CompilerParams(
            collective_id=0, has_side_effects=True, vmem_limit_bytes=66650000
        ),
        name="attention_layer",
    )(query_rows, key_rows, value_rows, log_decay, norm_gain.reshape(1, features), out_weight)


def solution(mesh):
    in_specs = (
        P("ctx", "tp"),
        P("ctx", "tp"),
        P("ctx", "tp"),
        P("tp", "ctx"),
        P("tp"),
        P(None, "tp"),
    )
    return jax.shard_map(
        per_device, mesh=mesh, in_specs=in_specs, out_specs=P("ctx", "tp"), check_vma=False
    )
```

```python
import functools

import jax
import jax.numpy as jnp
from jax import lax
from jax.experimental import pallas as pl
from jax.experimental.pallas import tpu as pltpu
from jax.sharding import PartitionSpec as P

HEADS = 32
HEAD_DIM = 128
MESH = pl.DeviceIdType.MESH
F32 = jnp.float32
BF16 = jnp.bfloat16
LANES = 128
NZ = 16
NY = 4
NX = 4
EARLY = 288
FAR = (8, 7, 9, 6, 10, 5, 11)
NEAR = (4, 12, 3, 13, 2, 14, 1, 15)
FAR_FIRST = FAR + NEAR


def dot(a, b, contract):
    return lax.dot_general(a, b, (contract, ((), ())), preferred_element_type=F32)


def column(row):
    return jnp.transpose(jnp.broadcast_to(row, (LANES, LANES)))


def kernel(
    q_hbm, k_hbm, v_hbm, ld_hbm, gain_hbm, w_hbm, out_hbm,
    out_ref, ld_ref, gain_ref, q_ref, k_ref, v_ref, w_ref, cum_ref, col_ref, att_ref, acc_ref,
    s_send, s_recv, d_send, d_recv, sf_ref, df_ref, p_ref, t_send, t_recv, e_send, e_recv,
    p_send, i_ref, qt_ref, al_ref, g_ref, a_ref, own_ref, sq_ref, ssq_ref,
    out_sem, load_sem, s_ssem, s_rsem, d_ssem, d_rsem, sf_ssem, sf_rsem, df_ssem, df_rsem, t_ssem, t_rsem, e_ssem, e_rsem,
    p_ssem, p_rsem, q_ssem, q_rsem, x_ssem, x_rsem,
):
    heads, length = ld_ref.shape
    tiles = length // LANES
    ctx = lax.axis_index("ctx")
    tp = lax.axis_index("tp")
    y, z = ctx // NZ, lax.rem(ctx, NZ)
    x, core = tp // 2, lax.rem(tp, 2)

    def tp_at(dx, other):
        cx = lax.rem(x + dx, NX)
        cc = 1 - core if other else core
        return cx * 2 + cc

    def z_peer(i):
        return y * NZ + lax.rem(z + i, NZ)

    def y_peer(i):
        return lax.rem(y + i, NY) * NZ + z

    loads = [
        pltpu.make_async_copy(src, dst, load_sem.at[n])
        for n, (src, dst) in enumerate(
            (
                (k_hbm, k_ref), (v_hbm, v_ref), (q_hbm, q_ref), (w_hbm, w_ref),
                (ld_hbm, ld_ref), (gain_hbm, gain_ref),
            )
        )
    ]
    for n in (4, 0, 1):
        loads[n].start()
    barrier = pltpu.get_barrier_semaphore()
    for i in NEAR:
        pl.semaphore_signal(barrier, inc=1, device_id={"ctx": z_peer(i)}, device_id_type=MESH)
    for i in (2, 1, 3):
        pl.semaphore_signal(barrier, inc=1, device_id={"ctx": y_peer(i)}, device_id_type=MESH)
    tp_peers = [tp_at(dx, other) for dx in range(NX) for other in (False, True)][1:]
    for peer in tp_peers:
        pl.semaphore_signal(barrier, inc=1, device_id={"tp": peer}, device_id_type=MESH)

    for n in (2, 5):
        loads[n].start()
    waiting = [4, 0, 1, 2, 5]
    sent = []

    def need(n):
        loads[n].wait()
        waiting.remove(n)

    def go(copy):
        copy.start()
        sent.append(copy)

    need(4)
    steps = jnp.concatenate(
        [ld_ref[:, b * LANES : (b + 1) * LANES] for b in range(tiles)]
        + ([] if heads * tiles % 8 == 0 else [jnp.zeros((8 - heads * tiles % 8, LANES), F32)]),
        axis=0,
    )
    lane = lax.broadcasted_iota(jnp.int32, steps.shape, 1)
    shift = 1
    while shift < LANES:
        steps = steps + jnp.where(lane >= shift, pltpu.roll(steps, shift, 1), 0.0)
        shift *= 2
    before = jnp.zeros((heads, LANES), F32)
    for b in range(tiles):
        part = steps[b * heads : (b + 1) * heads, :] + before
        cum_ref[b * heads : (b + 1) * heads, :] = part
        before = jnp.broadcast_to(part[:, LANES - 1 :], (heads, LANES))
    for h in range(heads):
        d_send[h] = before[h : h + 1, :]

    need(0)
    need(1)
    for h in range(heads):
        span = slice(h * LANES, (h + 1) * LANES)
        total = d_send[h]
        pieces = []
        for b in range(tiles):
            rows = slice(b * LANES, (b + 1) * LANES)
            col = column(cum_ref[b * heads + h : b * heads + h + 1, :])
            col_ref[h, rows, :] = col
            pieces.append((k_ref[rows, span].astype(F32) * jnp.exp(total - col)).astype(BF16))
        scaled = jnp.concatenate(pieces, axis=0)
        state = dot(scaled, v_ref[:, span], ((0,), (0,)))
        s_send[h * 4 : (h + 1) * 4] = state.astype(BF16).reshape(4, 32, LANES)

    pl.semaphore_wait(barrier, len(NEAR) + (NY - 1) + len(tp_peers))

    def s_copy(i):
        owner = lax.rem(z + i, NZ)
        return pltpu.make_async_remote_copy(
            src_ref=s_send.at[owner], dst_ref=s_recv.at[z], send_sem=s_ssem.at[i],
            recv_sem=s_rsem.at[i], device_id={"ctx": z_peer(i)}, device_id_type=MESH,
        )

    def d_copy(i):
        owner = lax.rem(z + i, NZ)
        return pltpu.make_async_remote_copy(
            src_ref=d_send.at[owner // 4], dst_ref=d_recv.at[z], send_sem=d_ssem.at[i],
            recv_sem=d_rsem.at[i], device_id={"ctx": z_peer(i)}, device_id_type=MESH,
        )

    def via(i):
        return 4 if i <= 8 else NZ - 4

    def s_out(i):
        return pltpu.make_async_remote_copy(
            src_ref=s_send.at[lax.rem(z + i, NZ)], dst_ref=sf_ref.at[i - 5],
            send_sem=s_ssem.at[i], recv_sem=sf_rsem.at[i - 5],
            device_id={"ctx": z_peer(via(i))}, device_id_type=MESH,
        )

    def d_out(i):
        return pltpu.make_async_remote_copy(
            src_ref=d_send.at[lax.rem(z + i, NZ) // 4], dst_ref=df_ref.at[i - 5],
            send_sem=d_ssem.at[i], recv_sem=df_rsem.at[i - 5],
            device_id={"ctx": z_peer(via(i))}, device_id_type=MESH,
        )

    def s_on(i):
        return pltpu.make_async_remote_copy(
            src_ref=sf_ref.at[i - 5], dst_ref=s_recv.at[lax.rem(z + NZ - via(i), NZ)],
            send_sem=sf_ssem.at[i - 5], recv_sem=s_rsem.at[i],
            device_id={"ctx": z_peer(NZ - via(i) + i)}, device_id_type=MESH,
        )

    def d_on(i):
        return pltpu.make_async_remote_copy(
            src_ref=df_ref.at[i - 5], dst_ref=d_recv.at[lax.rem(z + NZ - via(i), NZ)],
            send_sem=df_ssem.at[i - 5], recv_sem=d_rsem.at[i],
            device_id={"ctx": z_peer(NZ - via(i) + i)}, device_id_type=MESH,
        )

    for i in FAR:
        go(d_out(i))
        go(s_out(i))
    for i in NEAR:
        go(d_copy(i))
        go(s_copy(i))
    loads[3].start()
    waiting.append(3)
    s_recv[z] = s_send[z]
    d_recv[z] = d_send[z // 4]

    right, left, partner = tp_at(1, False), tp_at(NX - 1, False), tp_at(0, True)
    opposite = tp_at(2, False)
    right2, left2, opposite2 = tp_at(1, True), tp_at(NX - 1, True), tp_at(2, True)

    class Flow:
        def __init__(self, kind, ref):
            self.kind, self.ref, self.half, self.count = kind, ref, ref.shape[1] // 2, 0

        def copy(self, slot, part, peer, number):
            view = self.ref.at[slot, pl.ds(part * self.half, self.half)]
            return pltpu.make_async_remote_copy(
                src_ref=view, dst_ref=view, send_sem=x_ssem.at[self.kind, number],
                recv_sem=x_rsem.at[self.kind, slot, part], device_id={"tp": peer},
                device_id_type=MESH,
            )

        def start(self, slot, part, peer):
            go(self.copy(slot, part, peer, self.count))
            self.count += 1

        def arrive(self, slot, part):
            self.copy(slot, part, partner, 0).wait_recv()

        def own(self):
            for r, l in ((0, 1), (1, 0)):
                self.start(tp, r, right)
                self.start(tp, l, left)
            for part in (0, 1):
                self.start(tp, part, partner)

        def first(self):
            self.arrive(left, 0)
            self.start(left, 0, right)
            self.start(left, 0, partner)
            self.arrive(right, 1)
            self.start(right, 1, left)
            self.start(right, 1, partner)

        def second(self):
            self.arrive(left, 1)
            self.start(left, 1, partner)
            self.arrive(right, 0)
            self.start(right, 0, partner)

        def last(self):
            for part in (0, 1):
                self.arrive(opposite, part)
                self.start(opposite, part, partner)

        def near(self, slot):
            for part in (0, 1):
                self.arrive(slot, part)

    q_flow, al_flow, g_flow, a_flow = (
        Flow(n, ref) for n, ref in enumerate((qt_ref, al_ref, g_ref, a_ref))
    )
    need(2)
    for h in range(heads):
        span = slice(h * LANES, (h + 1) * LANES)
        growth = jnp.exp(col_ref[h, :EARLY, :])
        qt_ref[tp, :, span] = (q_ref[:EARLY, span].astype(F32) * growth).astype(BF16)

    q_flow.own()

    below = lax.broadcasted_iota(jnp.int32, (LANES, LANES), 0) >= lax.broadcasted_iota(
        jnp.int32, (LANES, LANES), 1
    )

    def inner_tile(h, b):
        span = slice(h * LANES, (h + 1) * LANES)
        rows = slice(b * LANES, (b + 1) * LANES)
        width = (b + 1) * LANES
        scores = dot(q_ref[rows, span], k_ref[:width, span], ((1,), (1,)))
        col = col_ref[h, rows, :]
        weights = []
        for s in range(b + 1):
            gap = col - cum_ref[s * heads + h : s * heads + h + 1, :]
            if s == b:
                factor = jnp.where(below, jnp.exp(jnp.where(below, gap, 0.0)), 0.0)
            else:
                factor = jnp.exp(gap)
            weights.append((scores[:, s * LANES : (s + 1) * LANES] * factor).astype(BF16))
        weight = weights[0] if b == 0 else jnp.concatenate(weights, axis=1)
        att_ref[rows, span] = dot(weight, v_ref[:width, span], ((1,), (0,)))

    for b in range(tiles):
        for h in range(heads):
            inner_tile(h, b)
    need(5)
    al_ref[tp] = (att_ref[:EARLY, :] * gain_ref[...]).astype(BF16)
    al_flow.own()

    for i in FAR:
        d_out(i).wait_recv()
        go(d_on(i))
        s_out(i).wait_recv()
        go(s_on(i))

    for i in FAR_FIRST:
        d_copy(i).wait_recv()
    log = jnp.zeros((1, LANES), F32)
    reach, decays = [], []
    for n in range(NZ):
        reach.append(jnp.exp(log))
        decays.append(jnp.exp(d_recv[n]))
        log = log + d_recv[n]
    e_send[...] = log

    def t_copy(i):
        return pltpu.make_async_remote_copy(
            src_ref=t_send, dst_ref=t_recv.at[y], send_sem=t_ssem.at[i],
            recv_sem=t_rsem.at[i], device_id={"ctx": y_peer(i)}, device_id_type=MESH,
        )

    def e_copy(i):
        return pltpu.make_async_remote_copy(
            src_ref=e_send, dst_ref=e_recv.at[y], send_sem=e_ssem.at[i],
            recv_sem=e_rsem.at[i], device_id={"ctx": y_peer(i)}, device_id_type=MESH,
        )

    for i in (2, 1, 3):
        go(e_copy(i))
    e_recv[y] = log
    for i in FAR_FIRST:
        s_copy(i).wait_recv()
    state = jnp.zeros((32, LANES), F32)
    prefixes = []
    for n in range(NZ):
        prefixes.append(state)
        state = decays[n] * state + s_recv[n].astype(F32)
    t_send[...] = state
    for i in (2, 1, 3):
        go(t_copy(i))
    t_recv[y] = state
    for n in range(NZ):
        p_ref[n] = prefixes[n]
    q_flow.first()
    for i in (1, 3, 2):
        e_copy(i).wait_recv()
    row_decays = [jnp.exp(e_recv[n]) for n in range(NY - 1)]
    for i in (1, 3, 2):
        t_copy(i).wait_recv()
    entering = jnp.zeros((32, LANES), F32)
    for n in range(NY - 1):
        entering = jnp.where(n < y, row_decays[n] * entering + t_recv[n], entering)

    def p_copy(i):
        return pltpu.make_async_remote_copy(
            src_ref=p_send.at[lax.rem(z + i, NZ)], dst_ref=i_ref.at[z], send_sem=p_ssem.at[i],
            recv_sem=p_rsem.at[i], device_id={"ctx": z_peer(i)}, device_id_type=MESH,
        )

    for n in range(NZ):
        p_send[n] = (p_ref[n] + reach[n] * entering).astype(BF16)
    for i in FAR_FIRST:
        go(p_copy(i))
    i_ref[z] = p_send[z]

    depth, width = a_ref.shape[2], out_ref.shape[1]
    early, late = slice(0, EARLY), slice(EARLY, length)

    def weight_of(slot):
        return w_ref[pl.ds(pl.multiple_of(slot * depth, depth), depth), :]

    def add(rows, block, slot):
        acc_ref[rows, :] += dot(block, weight_of(slot), ((1,), (0,)))

    def add_inner(slot):
        add(early, al_ref[slot], slot)

    def add_carried(slot):
        parts = []
        for h in range(heads):
            span = slice(h * LANES, (h + 1) * LANES)
            parts.append(
                dot(qt_ref[slot, :, span], g_ref[slot, span, :], ((1,), (0,))).astype(BF16)
            )
        add(early, jnp.concatenate(parts, axis=1), slot)

    def add_late(slot):
        add(late, a_ref[slot], slot)

    q_flow.second()
    acc_ref[...] = jnp.zeros_like(acc_ref)
    need(3)
    q_flow.near(partner)
    al_flow.near(partner)
    add_inner(partner)
    al_flow.first()
    al_flow.second()
    add_inner(left)
    add_inner(right)
    for slot in (left2, right2):
        q_flow.near(slot)
        al_flow.near(slot)
        add_inner(slot)
    q_flow.last()

    for i in FAR_FIRST:
        p_copy(i).wait_recv()
    for h in range(heads):
        span = slice(h * LANES, (h + 1) * LANES)
        state = i_ref[h * 4 : (h + 1) * 4].reshape(LANES, LANES).astype(F32)
        g_ref[tp, span, :] = (state * gain_ref[:, span]).astype(BF16)
    g_flow.own()

    def finish(rows, store):
        squares = None
        for h in range(heads):
            span = slice(h * LANES, (h + 1) * LANES)
            state = i_ref[h * 4 : (h + 1) * 4].reshape(LANES, LANES)
            carried = dot(q_ref[rows, span], state, ((1,), (0,))) * jnp.exp(col_ref[h, rows, :])
            value = att_ref[rows, span] + carried
            squares = value * value if squares is None else squares + value * value
            store(span, (value * gain_ref[:, span]).astype(BF16))
        sq_ref[rows, :] = squares

    def store_late(span, value):
        a_ref[tp, :, span] = value

    def store_own(span, value):
        own_ref[:, span] = value

    finish(late, store_late)
    a_flow.own()
    finish(early, store_own)
    for b in range(tiles):
        rows = slice(b * LANES, (b + 1) * LANES)
        ssq_ref[tp, :, rows] = jnp.sum(jnp.transpose(sq_ref[rows, :]), axis=0, keepdims=True)

    def ssq_copy(n):
        return pltpu.make_async_remote_copy(
            src_ref=ssq_ref.at[tp], dst_ref=ssq_ref.at[tp], send_sem=q_ssem.at[n],
            recv_sem=q_rsem.at[n], device_id={"tp": tp ^ (n + 1)}, device_id_type=MESH,
        )

    def ssq_from(n):
        slot = tp ^ (n + 1)
        return pltpu.make_async_remote_copy(
            src_ref=ssq_ref.at[slot], dst_ref=ssq_ref.at[slot], send_sem=q_ssem.at[n],
            recv_sem=q_rsem.at[n], device_id={"tp": slot}, device_id_type=MESH,
        )

    for n in range(7):
        go(ssq_copy(n))
    add(early, own_ref[...], tp)
    add_late(tp)
    g_flow.near(partner)
    add_carried(partner)
    g_flow.first()
    g_flow.second()
    al_flow.last()
    a_flow.near(partner)
    add_late(partner)
    add_carried(left)
    add_carried(right)
    a_flow.first()
    a_flow.second()
    add_late(left)
    add_late(right)
    g_flow.last()
    add_inner(opposite)
    add_carried(opposite)
    for n in range(7):
        ssq_from(n).wait_recv()
    squares = ssq_ref[0]
    for n in range(1, 8):
        squares = squares + ssq_ref[n]
    scale = lax.rsqrt(squares / (HEADS * HEAD_DIM) + 1e-06)
    for b in range(tiles):
        rows = slice(b * LANES, (b + 1) * LANES)
        sq_ref[rows, :] = column(scale[:, rows])

    def out_copy(rows, n):
        view = pl.ds(rows.start, rows.stop - rows.start)
        return pltpu.make_async_copy(out_ref.at[view], out_hbm.at[view], out_sem.at[n])

    def write(rows, n):
        out_ref[rows, :] = (
            acc_ref[rows, :] * jnp.tile(sq_ref[rows, :], (1, width // LANES))
        ).astype(BF16)
        out_copy(rows, n).start()

    for slot in (left2, right2, opposite2):
        if slot is opposite2:
            q_flow.near(slot)
            al_flow.near(slot)
            add_inner(slot)
        g_flow.near(slot)
        add_carried(slot)
        if slot is not opposite2:
            a_flow.near(slot)
            add_late(slot)
    write(early, 0)
    a_flow.last()
    add_late(opposite)
    a_flow.near(opposite2)
    add_late(opposite2)
    write(late, 1)

    for n in waiting:
        loads[n].wait()
    for copy in sent:
        copy.wait_send()
    out_copy(early, 0).wait()
    out_copy(late, 1).wait()


def per_device(query_rows, key_rows, value_rows, log_decay, norm_gain, out_weight):
    length, features = query_rows.shape
    heads = log_decay.shape[0]
    depth, width = out_weight.shape
    hbm = pl.BlockSpec(memory_space=pltpu.HBM)
    dma = pltpu.SemaphoreType.DMA
    return pl.pallas_call(
        kernel,
        out_shape=jax.ShapeDtypeStruct((length, width), BF16),
        in_specs=[hbm] * 6,
        out_specs=hbm,
        scratch_shapes=[
            pltpu.VMEM((length, width), BF16),
            pltpu.VMEM((heads, length), F32),
            pltpu.VMEM((1, features), F32),
            pltpu.VMEM((length, features), BF16),
            pltpu.VMEM((length, features), BF16),
            pltpu.VMEM((length, features), BF16),
            pltpu.VMEM((depth, width), BF16),
            pltpu.VMEM((16, LANES), F32),
            pltpu.VMEM((heads, length, LANES), F32),
            pltpu.VMEM((length, features), F32),
            pltpu.VMEM((length, width), F32),
            pltpu.VMEM((NZ, 32, LANES), BF16),
            pltpu.VMEM((NZ, 32, LANES), BF16),
            pltpu.VMEM((heads, 1, LANES), F32),
            pltpu.VMEM((NZ, 1, LANES), F32),
            pltpu.VMEM((7, 32, LANES), BF16),
            pltpu.VMEM((7, 1, LANES), F32),
            pltpu.VMEM((NZ, 32, LANES), F32),
            pltpu.VMEM((32, LANES), F32),
            pltpu.VMEM((NY, 32, LANES), F32),
            pltpu.VMEM((1, LANES), F32),
            pltpu.VMEM((NY, 1, LANES), F32),
            pltpu.VMEM((NZ, 32, LANES), BF16),
            pltpu.VMEM((NZ, 32, LANES), BF16),
            pltpu.VMEM((8, EARLY, features), BF16),
            pltpu.VMEM((8, EARLY, features), BF16),
            pltpu.VMEM((8, features, LANES), BF16),
            pltpu.VMEM((8, length - EARLY, features), BF16),
            pltpu.VMEM((EARLY, features), BF16),
            pltpu.VMEM((length, LANES), F32),
            pltpu.VMEM((8, 1, length), F32),
            dma((2,)), dma((6,)),
            dma((NZ,)), dma((NZ,)), dma((NZ,)), dma((NZ,)),
            dma((7,)), dma((7,)), dma((7,)), dma((7,)),
            dma((NY,)), dma((NY,)), dma((NY,)), dma((NY,)),
            dma((NZ,)), dma((NZ,)),
            dma((7,)), dma((7,)),
            dma((4, 14)), dma((4, 8, 2)),
        ],
        compiler_params=pltpu.CompilerParams(
            collective_id=0, has_side_effects=True, vmem_limit_bytes=66650000
        ),
        name="attention_layer",
    )(query_rows, key_rows, value_rows, log_decay, norm_gain.reshape(1, features), out_weight)


def solution(mesh):
    in_specs = (
        P("ctx", "tp"),
        P("ctx", "tp"),
        P("ctx", "tp"),
        P("tp", "ctx"),
        P("tp"),
        P(None, "tp"),
    )
    return jax.shard_map(
        per_device, mesh=mesh, in_specs=in_specs, out_specs=P("ctx", "tp"), check_vma=False
    )
```

```python
import functools

import jax
import jax.numpy as jnp
from jax import lax
from jax.experimental import pallas as pl
from jax.experimental.pallas import tpu as pltpu
from jax.sharding import PartitionSpec as P

HEADS = 32
HEAD_DIM = 128
MESH = pl.DeviceIdType.MESH
F32 = jnp.float32
BF16 = jnp.bfloat16
LANES = 128
NZ = 16
NY = 4
NX = 4
EARLY = 288
FAR = (8, 7, 9, 6, 10, 5, 11)
NEAR = (4, 12, 3, 13, 2, 14, 1, 15)
FAR_FIRST = FAR + NEAR


def dot(a, b, contract):
    return lax.dot_general(a, b, (contract, ((), ())), preferred_element_type=F32)


def column(row):
    return jnp.transpose(jnp.broadcast_to(row, (LANES, LANES)))


def kernel(
    q_hbm, k_hbm, v_hbm, ld_hbm, gain_hbm, w_hbm, out_hbm,
    out_ref, ld_ref, gain_ref, q_ref, k_ref, v_ref, w_ref, cum_ref, col_ref, att_ref, acc_ref,
    s_send, s_recv, d_send, d_recv, sf_ref, df_ref, p_ref, t_send, t_recv, e_send, e_recv,
    p_send, i_ref, qt_ref, al_ref, g_ref, a_ref, own_ref, sq_ref, ssq_ref,
    out_sem, load_sem, s_ssem, s_rsem, d_ssem, d_rsem, sf_ssem, sf_rsem, df_ssem, df_rsem, t_ssem, t_rsem, e_ssem, e_rsem,
    p_ssem, p_rsem, q_ssem, q_rsem, x_ssem, x_rsem,
):
    heads, length = ld_ref.shape
    tiles = length // LANES
    ctx = lax.axis_index("ctx")
    tp = lax.axis_index("tp")
    y, z = ctx // NZ, lax.rem(ctx, NZ)
    x, core = tp // 2, lax.rem(tp, 2)

    def tp_at(dx, other):
        cx = lax.rem(x + dx, NX)
        cc = 1 - core if other else core
        return cx * 2 + cc

    def z_peer(i):
        return y * NZ + lax.rem(z + i, NZ)

    def y_peer(i):
        return lax.rem(y + i, NY) * NZ + z

    loads = [
        pltpu.make_async_copy(src, dst, load_sem.at[n])
        for n, (src, dst) in enumerate(
            (
                (k_hbm, k_ref), (v_hbm, v_ref), (q_hbm, q_ref), (w_hbm, w_ref),
                (ld_hbm, ld_ref), (gain_hbm, gain_ref),
            )
        )
    ]
    for n in (4, 0, 1):
        loads[n].start()
    barrier = pltpu.get_barrier_semaphore()
    for i in NEAR:
        pl.semaphore_signal(barrier, inc=1, device_id={"ctx": z_peer(i)}, device_id_type=MESH)
    for i in (2, 1, 3):
        pl.semaphore_signal(barrier, inc=1, device_id={"ctx": y_peer(i)}, device_id_type=MESH)
    tp_peers = [tp_at(dx, other) for dx in range(NX) for other in (False, True)][1:]
    for peer in tp_peers:
        pl.semaphore_signal(barrier, inc=1, device_id={"tp": peer}, device_id_type=MESH)

    for n in (2, 5):
        loads[n].start()
    waiting = [4, 0, 1, 2, 5]
    sent = []

    def need(n):
        loads[n].wait()
        waiting.remove(n)

    def go(copy):
        copy.start()
        sent.append(copy)

    need(4)
    steps = jnp.concatenate(
        [ld_ref[:, b * LANES : (b + 1) * LANES] for b in range(tiles)]
        + ([] if heads * tiles % 8 == 0 else [jnp.zeros((8 - heads * tiles % 8, LANES), F32)]),
        axis=0,
    )
    lane = lax.broadcasted_iota(jnp.int32, steps.shape, 1)
    shift = 1
    while shift < LANES:
        steps = steps + jnp.where(lane >= shift, pltpu.roll(steps, shift, 1), 0.0)
        shift *= 2
    before = jnp.zeros((heads, LANES), F32)
    for b in range(tiles):
        part = steps[b * heads : (b + 1) * heads, :] + before
        cum_ref[b * heads : (b + 1) * heads, :] = part
        before = jnp.broadcast_to(part[:, LANES - 1 :], (heads, LANES))
    for h in range(heads):
        d_send[h] = before[h : h + 1, :]

    need(0)
    need(1)
    for h in range(heads):
        span = slice(h * LANES, (h + 1) * LANES)
        total = d_send[h]
        pieces = []
        for b in range(tiles):
            rows = slice(b * LANES, (b + 1) * LANES)
            col = column(cum_ref[b * heads + h : b * heads + h + 1, :])
            col_ref[h, rows, :] = col
            pieces.append((k_ref[rows, span].astype(F32) * jnp.exp(total - col)).astype(BF16))
        scaled = jnp.concatenate(pieces, axis=0)
        state = dot(scaled, v_ref[:, span], ((0,), (0,)))
        s_send[h * 4 : (h + 1) * 4] = state.astype(BF16).reshape(4, 32, LANES)

    pl.semaphore_wait(barrier, len(NEAR) + (NY - 1) + len(tp_peers))

    def s_copy(i):
        owner = lax.rem(z + i, NZ)
        return pltpu.make_async_remote_copy(
            src_ref=s_send.at[owner], dst_ref=s_recv.at[z], send_sem=s_ssem.at[i],
            recv_sem=s_rsem.at[i], device_id={"ctx": z_peer(i)}, device_id_type=MESH,
        )

    def d_copy(i):
        owner = lax.rem(z + i, NZ)
        return pltpu.make_async_remote_copy(
            src_ref=d_send.at[owner // 4], dst_ref=d_recv.at[z], send_sem=d_ssem.at[i],
            recv_sem=d_rsem.at[i], device_id={"ctx": z_peer(i)}, device_id_type=MESH,
        )

    def via(i):
        return 4 if i <= 8 else NZ - 4

    def s_out(i):
        return pltpu.make_async_remote_copy(
            src_ref=s_send.at[lax.rem(z + i, NZ)], dst_ref=sf_ref.at[i - 5],
            send_sem=s_ssem.at[i], recv_sem=sf_rsem.at[i - 5],
            device_id={"ctx": z_peer(via(i))}, device_id_type=MESH,
        )

    def d_out(i):
        return pltpu.make_async_remote_copy(
            src_ref=d_send.at[lax.rem(z + i, NZ) // 4], dst_ref=df_ref.at[i - 5],
            send_sem=d_ssem.at[i], recv_sem=df_rsem.at[i - 5],
            device_id={"ctx": z_peer(via(i))}, device_id_type=MESH,
        )

    def s_on(i):
        return pltpu.make_async_remote_copy(
            src_ref=sf_ref.at[i - 5], dst_ref=s_recv.at[lax.rem(z + NZ - via(i), NZ)],
            send_sem=sf_ssem.at[i - 5], recv_sem=s_rsem.at[i],
            device_id={"ctx": z_peer(NZ - via(i) + i)}, device_id_type=MESH,
        )

    def d_on(i):
        return pltpu.make_async_remote_copy(
            src_ref=df_ref.at[i - 5], dst_ref=d_recv.at[lax.rem(z + NZ - via(i), NZ)],
            send_sem=df_ssem.at[i - 5], recv_sem=d_rsem.at[i],
            device_id={"ctx": z_peer(NZ - via(i) + i)}, device_id_type=MESH,
        )

    for i in FAR:
        go(d_out(i))
        go(s_out(i))
    for i in NEAR:
        go(d_copy(i))
        go(s_copy(i))
    loads[3].start()
    waiting.append(3)
    s_recv[z] = s_send[z]
    d_recv[z] = d_send[z // 4]

    right, left, partner = tp_at(1, False), tp_at(NX - 1, False), tp_at(0, True)
    opposite = tp_at(2, False)
    right2, left2, opposite2 = tp_at(1, True), tp_at(NX - 1, True), tp_at(2, True)

    class Flow:
        def __init__(self, kind, ref):
            self.kind, self.ref, self.half, self.count = kind, ref, ref.shape[1] // 2, 0

        def copy(self, slot, part, peer, number):
            view = self.ref.at[slot, pl.ds(part * self.half, self.half)]
            return pltpu.make_async_remote_copy(
                src_ref=view, dst_ref=view, send_sem=x_ssem.at[self.kind, number],
                recv_sem=x_rsem.at[self.kind, slot, part], device_id={"tp": peer},
                device_id_type=MESH,
            )

        def start(self, slot, part, peer):
            go(self.copy(slot, part, peer, self.count))
            self.count += 1

        def arrive(self, slot, part):
            self.copy(slot, part, partner, 0).wait_recv()

        def own(self):
            for r, l in ((0, 1), (1, 0)):
                self.start(tp, r, right)
                self.start(tp, l, left)
            for part in (0, 1):
                self.start(tp, part, partner)

        def first(self):
            self.arrive(left, 0)
            self.start(left, 0, right)
            self.start(left, 0, partner)
            self.arrive(right, 1)
            self.start(right, 1, left)
            self.start(right, 1, partner)

        def second(self):
            self.arrive(left, 1)
            self.start(left, 1, partner)
            self.arrive(right, 0)
            self.start(right, 0, partner)

        def last(self):
            for part in (0, 1):
                self.arrive(opposite, part)
                self.start(opposite, part, partner)

        def near(self, slot):
            for part in (0, 1):
                self.arrive(slot, part)

    q_flow, al_flow, g_flow, a_flow = (
        Flow(n, ref) for n, ref in enumerate((qt_ref, al_ref, g_ref, a_ref))
    )
    need(2)
    for h in range(heads):
        span = slice(h * LANES, (h + 1) * LANES)
        growth = jnp.exp(col_ref[h, :EARLY, :])
        qt_ref[tp, :, span] = (q_ref[:EARLY, span].astype(F32) * growth).astype(BF16)

    q_flow.own()

    below = lax.broadcasted_iota(jnp.int32, (LANES, LANES), 0) >= lax.broadcasted_iota(
        jnp.int32, (LANES, LANES), 1
    )

    def inner_tile(h, b):
        span = slice(h * LANES, (h + 1) * LANES)
        rows = slice(b * LANES, (b + 1) * LANES)
        width = (b + 1) * LANES
        scores = dot(q_ref[rows, span], k_ref[:width, span], ((1,), (1,)))
        col = col_ref[h, rows, :]
        weights = []
        for s in range(b + 1):
            gap = col - cum_ref[s * heads + h : s * heads + h + 1, :]
            if s == b:
                factor = jnp.where(below, jnp.exp(jnp.where(below, gap, 0.0)), 0.0)
            else:
                factor = jnp.exp(gap)
            weights.append((scores[:, s * LANES : (s + 1) * LANES] * factor).astype(BF16))
        weight = weights[0] if b == 0 else jnp.concatenate(weights, axis=1)
        att_ref[rows, span] = dot(weight, v_ref[:width, span], ((1,), (0,)))

    for b in range(tiles):
        for h in range(heads):
            inner_tile(h, b)
    need(5)
    al_ref[tp] = (att_ref[:EARLY, :] * gain_ref[...]).astype(BF16)
    al_flow.own()

    for i in FAR:
        d_out(i).wait_recv()
        go(d_on(i))
        s_out(i).wait_recv()
        go(s_on(i))

    for i in FAR_FIRST:
        d_copy(i).wait_recv()
    log = jnp.zeros((1, LANES), F32)
    reach, decays = [], []
    for n in range(NZ):
        reach.append(jnp.exp(log))
        decays.append(jnp.exp(d_recv[n]))
        log = log + d_recv[n]
    e_send[...] = log

    def t_copy(i):
        return pltpu.make_async_remote_copy(
            src_ref=t_send, dst_ref=t_recv.at[y], send_sem=t_ssem.at[i],
            recv_sem=t_rsem.at[i], device_id={"ctx": y_peer(i)}, device_id_type=MESH,
        )

    def e_copy(i):
        return pltpu.make_async_remote_copy(
            src_ref=e_send, dst_ref=e_recv.at[y], send_sem=e_ssem.at[i],
            recv_sem=e_rsem.at[i], device_id={"ctx": y_peer(i)}, device_id_type=MESH,
        )

    for i in (2, 1, 3):
        go(e_copy(i))
    e_recv[y] = log
    for i in FAR_FIRST:
        s_copy(i).wait_recv()
    state = jnp.zeros((32, LANES), F32)
    prefixes = []
    for n in range(NZ):
        prefixes.append(state)
        state = decays[n] * state + s_recv[n].astype(F32)
    t_send[...] = state
    for i in (2, 1, 3):
        go(t_copy(i))
    t_recv[y] = state
    for n in range(NZ):
        p_ref[n] = prefixes[n]
    q_flow.first()
    for i in (1, 3, 2):
        e_copy(i).wait_recv()
    row_decays = [jnp.exp(e_recv[n]) for n in range(NY - 1)]
    for i in (1, 3, 2):
        t_copy(i).wait_recv()
    entering = jnp.zeros((32, LANES), F32)
    for n in range(NY - 1):
        entering = jnp.where(n < y, row_decays[n] * entering + t_recv[n], entering)

    def p_copy(i):
        return pltpu.make_async_remote_copy(
            src_ref=p_send.at[lax.rem(z + i, NZ)], dst_ref=i_ref.at[z], send_sem=p_ssem.at[i],
            recv_sem=p_rsem.at[i], device_id={"ctx": z_peer(i)}, device_id_type=MESH,
        )

    for n in range(NZ):
        p_send[n] = (p_ref[n] + reach[n] * entering).astype(BF16)
    for i in FAR_FIRST:
        go(p_copy(i))
    i_ref[z] = p_send[z]

    depth, width = a_ref.shape[2], out_ref.shape[1]
    early, late = slice(0, EARLY), slice(EARLY, length)

    def weight_of(slot):
        return w_ref[pl.ds(pl.multiple_of(slot * depth, depth), depth), :]

    def add(rows, block, slot):
        acc_ref[rows, :] += dot(block, weight_of(slot), ((1,), (0,)))

    def add_inner(slot):
        add(early, al_ref[slot], slot)

    def add_carried(slot):
        parts = []
        for h in range(heads):
            span = slice(h * LANES, (h + 1) * LANES)
            parts.append(
                dot(qt_ref[slot, :, span], g_ref[slot, span, :], ((1,), (0,))).astype(BF16)
            )
        add(early, jnp.concatenate(parts, axis=1), slot)

    def add_late(slot):
        add(late, a_ref[slot], slot)

    q_flow.second()
    acc_ref[...] = jnp.zeros_like(acc_ref)
    need(3)
    q_flow.near(partner)
    al_flow.near(partner)
    add_inner(partner)
    al_flow.first()
    al_flow.second()
    add_inner(left)
    add_inner(right)
    for slot in (left2, right2):
        q_flow.near(slot)
        al_flow.near(slot)
        add_inner(slot)
    q_flow.last()

    for i in FAR_FIRST:
        p_copy(i).wait_recv()
    for h in range(heads):
        span = slice(h * LANES, (h + 1) * LANES)
        state = i_ref[h * 4 : (h + 1) * 4].reshape(LANES, LANES).astype(F32)
        g_ref[tp, span, :] = (state * gain_ref[:, span]).astype(BF16)
    g_flow.own()

    def finish(rows, store):
        squares = None
        for h in range(heads):
            span = slice(h * LANES, (h + 1) * LANES)
            state = i_ref[h * 4 : (h + 1) * 4].reshape(LANES, LANES)
            carried = dot(q_ref[rows, span], state, ((1,), (0,))) * jnp.exp(col_ref[h, rows, :])
            value = att_ref[rows, span] + carried
            squares = value * value if squares is None else squares + value * value
            store(span, (value * gain_ref[:, span]).astype(BF16))
        sq_ref[rows, :] = squares

    def store_late(span, value):
        a_ref[tp, :, span] = value

    def store_own(span, value):
        own_ref[:, span] = value

    finish(late, store_late)
    a_flow.own()
    finish(early, store_own)
    for b in range(tiles):
        rows = slice(b * LANES, (b + 1) * LANES)
        ssq_ref[tp, :, rows] = jnp.sum(jnp.transpose(sq_ref[rows, :]), axis=0, keepdims=True)

    def ssq_copy(n):
        return pltpu.make_async_remote_copy(
            src_ref=ssq_ref.at[tp], dst_ref=ssq_ref.at[tp], send_sem=q_ssem.at[n],
            recv_sem=q_rsem.at[n], device_id={"tp": tp ^ (n + 1)}, device_id_type=MESH,
        )

    def ssq_from(n):
        slot = tp ^ (n + 1)
        return pltpu.make_async_remote_copy(
            src_ref=ssq_ref.at[slot], dst_ref=ssq_ref.at[slot], send_sem=q_ssem.at[n],
            recv_sem=q_rsem.at[n], device_id={"tp": slot}, device_id_type=MESH,
        )

    for n in range(7):
        go(ssq_copy(n))
    add(early, own_ref[...], tp)
    add_late(tp)
    g_flow.near(partner)
    add_carried(partner)
    g_flow.first()
    g_flow.second()
    al_flow.last()
    a_flow.near(partner)
    add_late(partner)
    a_flow.first()
    add_carried(left)
    add_carried(right)
    a_flow.second()
    add_late(left)
    add_late(right)
    g_flow.last()
    add_inner(opposite)
    add_carried(opposite)
    for n in range(7):
        ssq_from(n).wait_recv()
    squares = ssq_ref[0]
    for n in range(1, 8):
        squares = squares + ssq_ref[n]
    scale = lax.rsqrt(squares / (HEADS * HEAD_DIM) + 1e-06)
    for b in range(tiles):
        rows = slice(b * LANES, (b + 1) * LANES)
        sq_ref[rows, :] = column(scale[:, rows])

    def out_copy(rows, n):
        view = pl.ds(rows.start, rows.stop - rows.start)
        return pltpu.make_async_copy(out_ref.at[view], out_hbm.at[view], out_sem.at[n])

    def write(rows, n):
        out_ref[rows, :] = (
            acc_ref[rows, :] * jnp.tile(sq_ref[rows, :], (1, width // LANES))
        ).astype(BF16)
        out_copy(rows, n).start()

    for slot in (left2, right2, opposite2):
        if slot is opposite2:
            q_flow.near(slot)
            al_flow.near(slot)
            add_inner(slot)
        g_flow.near(slot)
        add_carried(slot)
        if slot is not opposite2:
            a_flow.near(slot)
            add_late(slot)
    write(early, 0)
    a_flow.last()
    add_late(opposite)
    a_flow.near(opposite2)
    add_late(opposite2)
    write(late, 1)

    for n in waiting:
        loads[n].wait()
    for copy in sent:
        copy.wait_send()
    out_copy(early, 0).wait()
    out_copy(late, 1).wait()


def per_device(query_rows, key_rows, value_rows, log_decay, norm_gain, out_weight):
    length, features = query_rows.shape
    heads = log_decay.shape[0]
    depth, width = out_weight.shape
    hbm = pl.BlockSpec(memory_space=pltpu.HBM)
    dma = pltpu.SemaphoreType.DMA
    return pl.pallas_call(
        kernel,
        out_shape=jax.ShapeDtypeStruct((length, width), BF16),
        in_specs=[hbm] * 6,
        out_specs=hbm,
        scratch_shapes=[
            pltpu.VMEM((length, width), BF16),
            pltpu.VMEM((heads, length), F32),
            pltpu.VMEM((1, features), F32),
            pltpu.VMEM((length, features), BF16),
            pltpu.VMEM((length, features), BF16),
            pltpu.VMEM((length, features), BF16),
            pltpu.VMEM((depth, width), BF16),
            pltpu.VMEM((16, LANES), F32),
            pltpu.VMEM((heads, length, LANES), F32),
            pltpu.VMEM((length, features), F32),
            pltpu.VMEM((length, width), F32),
            pltpu.VMEM((NZ, 32, LANES), BF16),
            pltpu.VMEM((NZ, 32, LANES), BF16),
            pltpu.VMEM((heads, 1, LANES), F32),
            pltpu.VMEM((NZ, 1, LANES), F32),
            pltpu.VMEM((7, 32, LANES), BF16),
            pltpu.VMEM((7, 1, LANES), F32),
            pltpu.VMEM((NZ, 32, LANES), F32),
            pltpu.VMEM((32, LANES), F32),
            pltpu.VMEM((NY, 32, LANES), F32),
            pltpu.VMEM((1, LANES), F32),
            pltpu.VMEM((NY, 1, LANES), F32),
            pltpu.VMEM((NZ, 32, LANES), BF16),
            pltpu.VMEM((NZ, 32, LANES), BF16),
            pltpu.VMEM((8, EARLY, features), BF16),
            pltpu.VMEM((8, EARLY, features), BF16),
            pltpu.VMEM((8, features, LANES), BF16),
            pltpu.VMEM((8, length - EARLY, features), BF16),
            pltpu.VMEM((EARLY, features), BF16),
            pltpu.VMEM((length, LANES), F32),
            pltpu.VMEM((8, 1, length), F32),
            dma((2,)), dma((6,)),
            dma((NZ,)), dma((NZ,)), dma((NZ,)), dma((NZ,)),
            dma((7,)), dma((7,)), dma((7,)), dma((7,)),
            dma((NY,)), dma((NY,)), dma((NY,)), dma((NY,)),
            dma((NZ,)), dma((NZ,)),
            dma((7,)), dma((7,)),
            dma((4, 14)), dma((4, 8, 2)),
        ],
        compiler_params=pltpu.CompilerParams(
            collective_id=0, has_side_effects=True, vmem_limit_bytes=66650000
        ),
        name="attention_layer",
    )(query_rows, key_rows, value_rows, log_decay, norm_gain.reshape(1, features), out_weight)


def solution(mesh):
    in_specs = (
        P("ctx", "tp"),
        P("ctx", "tp"),
        P("ctx", "tp"),
        P("tp", "ctx"),
        P("tp"),
        P(None, "tp"),
    )
    return jax.shard_map(
        per_device, mesh=mesh, in_specs=in_specs, out_specs=P("ctx", "tp"), check_vma=False
    )
```

```python
import functools

import jax
import jax.numpy as jnp
from jax import lax
from jax.experimental import pallas as pl
from jax.experimental.pallas import tpu as pltpu
from jax.sharding import PartitionSpec as P

HEADS = 32
HEAD_DIM = 128
MESH = pl.DeviceIdType.MESH
F32 = jnp.float32
BF16 = jnp.bfloat16
LANES = 128
NZ = 16
NY = 4
NX = 4
EARLY = 320
FAR = (8, 7, 9, 6, 10, 5, 11)
NEAR = (4, 12, 3, 13, 2, 14, 1, 15)
FAR_FIRST = FAR + NEAR


def dot(a, b, contract):
    return lax.dot_general(a, b, (contract, ((), ())), preferred_element_type=F32)


def column(row):
    return jnp.transpose(jnp.broadcast_to(row, (LANES, LANES)))


def kernel(
    q_hbm, k_hbm, v_hbm, ld_hbm, gain_hbm, w_hbm, out_hbm,
    out_ref, ld_ref, gain_ref, q_ref, k_ref, v_ref, w_ref, cum_ref, col_ref, att_ref, acc_ref,
    s_send, s_recv, d_send, d_recv, sf_ref, df_ref, p_ref, t_send, t_recv, e_send, e_recv,
    p_send, i_ref, qt_ref, al_ref, g_ref, a_ref, own_ref, sq_ref, ssq_ref,
    out_sem, load_sem, s_ssem, s_rsem, d_ssem, d_rsem, sf_ssem, sf_rsem, df_ssem, df_rsem, t_ssem, t_rsem, e_ssem, e_rsem,
    p_ssem, p_rsem, q_ssem, q_rsem, x_ssem, x_rsem,
):
    heads, length = ld_ref.shape
    tiles = length // LANES
    ctx = lax.axis_index("ctx")
    tp = lax.axis_index("tp")
    y, z = ctx // NZ, lax.rem(ctx, NZ)
    x, core = tp // 2, lax.rem(tp, 2)

    def tp_at(dx, other):
        cx = lax.rem(x + dx, NX)
        cc = 1 - core if other else core
        return cx * 2 + cc

    def z_peer(i):
        return y * NZ + lax.rem(z + i, NZ)

    def y_peer(i):
        return lax.rem(y + i, NY) * NZ + z

    loads = [
        pltpu.make_async_copy(src, dst, load_sem.at[n])
        for n, (src, dst) in enumerate(
            (
                (k_hbm, k_ref), (v_hbm, v_ref), (q_hbm, q_ref), (w_hbm, w_ref),
                (ld_hbm, ld_ref), (gain_hbm, gain_ref),
            )
        )
    ]
    for n in (4, 0, 1):
        loads[n].start()
    barrier = pltpu.get_barrier_semaphore()
    for i in NEAR:
        pl.semaphore_signal(barrier, inc=1, device_id={"ctx": z_peer(i)}, device_id_type=MESH)
    for i in (2, 1, 3):
        pl.semaphore_signal(barrier, inc=1, device_id={"ctx": y_peer(i)}, device_id_type=MESH)
    tp_peers = [tp_at(dx, other) for dx in range(NX) for other in (False, True)][1:]
    for peer in tp_peers:
        pl.semaphore_signal(barrier, inc=1, device_id={"tp": peer}, device_id_type=MESH)

    for n in (2, 5):
        loads[n].start()
    waiting = [4, 0, 1, 2, 5]
    sent = []

    def need(n):
        loads[n].wait()
        waiting.remove(n)

    def go(copy):
        copy.start()
        sent.append(copy)

    need(4)
    steps = jnp.concatenate(
        [ld_ref[:, b * LANES : (b + 1) * LANES] for b in range(tiles)]
        + ([] if heads * tiles % 8 == 0 else [jnp.zeros((8 - heads * tiles % 8, LANES), F32)]),
        axis=0,
    )
    lane = lax.broadcasted_iota(jnp.int32, steps.shape, 1)
    shift = 1
    while shift < LANES:
        steps = steps + jnp.where(lane >= shift, pltpu.roll(steps, shift, 1), 0.0)
        shift *= 2
    before = jnp.zeros((heads, LANES), F32)
    for b in range(tiles):
        part = steps[b * heads : (b + 1) * heads, :] + before
        cum_ref[b * heads : (b + 1) * heads, :] = part
        before = jnp.broadcast_to(part[:, LANES - 1 :], (heads, LANES))
    for h in range(heads):
        d_send[h] = before[h : h + 1, :]

    need(0)
    need(1)
    for h in range(heads):
        span = slice(h * LANES, (h + 1) * LANES)
        total = d_send[h]
        pieces = []
        for b in range(tiles):
            rows = slice(b * LANES, (b + 1) * LANES)
            col = column(cum_ref[b * heads + h : b * heads + h + 1, :])
            col_ref[h, rows, :] = col
            pieces.append((k_ref[rows, span].astype(F32) * jnp.exp(total - col)).astype(BF16))
        scaled = jnp.concatenate(pieces, axis=0)
        state = dot(scaled, v_ref[:, span], ((0,), (0,)))
        s_send[h * 4 : (h + 1) * 4] = state.astype(BF16).reshape(4, 32, LANES)

    pl.semaphore_wait(barrier, len(NEAR) + (NY - 1) + len(tp_peers))

    def s_copy(i):
        owner = lax.rem(z + i, NZ)
        return pltpu.make_async_remote_copy(
            src_ref=s_send.at[owner], dst_ref=s_recv.at[z], send_sem=s_ssem.at[i],
            recv_sem=s_rsem.at[i], device_id={"ctx": z_peer(i)}, device_id_type=MESH,
        )

    def d_copy(i):
        owner = lax.rem(z + i, NZ)
        return pltpu.make_async_remote_copy(
            src_ref=d_send.at[owner // 4], dst_ref=d_recv.at[z], send_sem=d_ssem.at[i],
            recv_sem=d_rsem.at[i], device_id={"ctx": z_peer(i)}, device_id_type=MESH,
        )

    def via(i):
        return 4 if i <= 8 else NZ - 4

    def s_out(i):
        return pltpu.make_async_remote_copy(
            src_ref=s_send.at[lax.rem(z + i, NZ)], dst_ref=sf_ref.at[i - 5],
            send_sem=s_ssem.at[i], recv_sem=sf_rsem.at[i - 5],
            device_id={"ctx": z_peer(via(i))}, device_id_type=MESH,
        )

    def d_out(i):
        return pltpu.make_async_remote_copy(
            src_ref=d_send.at[lax.rem(z + i, NZ) // 4], dst_ref=df_ref.at[i - 5],
            send_sem=d_ssem.at[i], recv_sem=df_rsem.at[i - 5],
            device_id={"ctx": z_peer(via(i))}, device_id_type=MESH,
        )

    def s_on(i):
        return pltpu.make_async_remote_copy(
            src_ref=sf_ref.at[i - 5], dst_ref=s_recv.at[lax.rem(z + NZ - via(i), NZ)],
            send_sem=sf_ssem.at[i - 5], recv_sem=s_rsem.at[i],
            device_id={"ctx": z_peer(NZ - via(i) + i)}, device_id_type=MESH,
        )

    def d_on(i):
        return pltpu.make_async_remote_copy(
            src_ref=df_ref.at[i - 5], dst_ref=d_recv.at[lax.rem(z + NZ - via(i), NZ)],
            send_sem=df_ssem.at[i - 5], recv_sem=d_rsem.at[i],
            device_id={"ctx": z_peer(NZ - via(i) + i)}, device_id_type=MESH,
        )

    for i in FAR:
        go(d_out(i))
        go(s_out(i))
    for i in NEAR:
        go(d_copy(i))
        go(s_copy(i))
    loads[3].start()
    waiting.append(3)
    s_recv[z] = s_send[z]
    d_recv[z] = d_send[z // 4]

    right, left, partner = tp_at(1, False), tp_at(NX - 1, False), tp_at(0, True)
    opposite = tp_at(2, False)
    right2, left2, opposite2 = tp_at(1, True), tp_at(NX - 1, True), tp_at(2, True)

    class Flow:
        def __init__(self, kind, ref):
            self.kind, self.ref, self.half, self.count = kind, ref, ref.shape[1] // 2, 0

        def copy(self, slot, part, peer, number):
            view = self.ref.at[slot, pl.ds(part * self.half, self.half)]
            return pltpu.make_async_remote_copy(
                src_ref=view, dst_ref=view, send_sem=x_ssem.at[self.kind, number],
                recv_sem=x_rsem.at[self.kind, slot, part], device_id={"tp": peer},
                device_id_type=MESH,
            )

        def start(self, slot, part, peer):
            go(self.copy(slot, part, peer, self.count))
            self.count += 1

        def arrive(self, slot, part):
            self.copy(slot, part, partner, 0).wait_recv()

        def own(self):
            for r, l in ((0, 1), (1, 0)):
                self.start(tp, r, right)
                self.start(tp, l, left)
            for part in (0, 1):
                self.start(tp, part, partner)

        def first(self):
            self.arrive(left, 0)
            self.start(left, 0, right)
            self.start(left, 0, partner)
            self.arrive(right, 1)
            self.start(right, 1, left)
            self.start(right, 1, partner)

        def second(self):
            self.arrive(left, 1)
            self.start(left, 1, partner)
            self.arrive(right, 0)
            self.start(right, 0, partner)

        def last(self):
            for part in (0, 1):
                self.arrive(opposite, part)
                self.start(opposite, part, partner)

        def near(self, slot):
            for part in (0, 1):
                self.arrive(slot, part)

    q_flow, al_flow, g_flow, a_flow = (
        Flow(n, ref) for n, ref in enumerate((qt_ref, al_ref, g_ref, a_ref))
    )
    need(2)
    for h in range(heads):
        span = slice(h * LANES, (h + 1) * LANES)
        growth = jnp.exp(col_ref[h, :EARLY, :])
        qt_ref[tp, :, span] = (q_ref[:EARLY, span].astype(F32) * growth).astype(BF16)

    q_flow.own()

    below = lax.broadcasted_iota(jnp.int32, (LANES, LANES), 0) >= lax.broadcasted_iota(
        jnp.int32, (LANES, LANES), 1
    )

    def inner_tile(h, b):
        span = slice(h * LANES, (h + 1) * LANES)
        rows = slice(b * LANES, (b + 1) * LANES)
        width = (b + 1) * LANES
        scores = dot(q_ref[rows, span], k_ref[:width, span], ((1,), (1,)))
        col = col_ref[h, rows, :]
        weights = []
        for s in range(b + 1):
            gap = col - cum_ref[s * heads + h : s * heads + h + 1, :]
            if s == b:
                factor = jnp.where(below, jnp.exp(jnp.where(below, gap, 0.0)), 0.0)
            else:
                factor = jnp.exp(gap)
            weights.append((scores[:, s * LANES : (s + 1) * LANES] * factor).astype(BF16))
        weight = weights[0] if b == 0 else jnp.concatenate(weights, axis=1)
        att_ref[rows, span] = dot(weight, v_ref[:width, span], ((1,), (0,)))

    for b in range(tiles):
        for h in range(heads):
            inner_tile(h, b)
    need(5)
    al_ref[tp] = (att_ref[:EARLY, :] * gain_ref[...]).astype(BF16)
    al_flow.own()

    for i in FAR:
        d_out(i).wait_recv()
        go(d_on(i))
        s_out(i).wait_recv()
        go(s_on(i))

    for i in FAR_FIRST:
        d_copy(i).wait_recv()
    log = jnp.zeros((1, LANES), F32)
    reach, decays = [], []
    for n in range(NZ):
        reach.append(jnp.exp(log))
        decays.append(jnp.exp(d_recv[n]))
        log = log + d_recv[n]
    e_send[...] = log

    def t_copy(i):
        return pltpu.make_async_remote_copy(
            src_ref=t_send, dst_ref=t_recv.at[y], send_sem=t_ssem.at[i],
            recv_sem=t_rsem.at[i], device_id={"ctx": y_peer(i)}, device_id_type=MESH,
        )

    def e_copy(i):
        return pltpu.make_async_remote_copy(
            src_ref=e_send, dst_ref=e_recv.at[y], send_sem=e_ssem.at[i],
            recv_sem=e_rsem.at[i], device_id={"ctx": y_peer(i)}, device_id_type=MESH,
        )

    for i in (2, 1, 3):
        go(e_copy(i))
    e_recv[y] = log
    for i in FAR_FIRST:
        s_copy(i).wait_recv()
    state = jnp.zeros((32, LANES), F32)
    prefixes = []
    for n in range(NZ):
        prefixes.append(state)
        state = decays[n] * state + s_recv[n].astype(F32)
    t_send[...] = state
    for i in (2, 1, 3):
        go(t_copy(i))
    t_recv[y] = state
    for n in range(NZ):
        p_ref[n] = prefixes[n]
    q_flow.first()
    for i in (1, 3, 2):
        e_copy(i).wait_recv()
    row_decays = [jnp.exp(e_recv[n]) for n in range(NY - 1)]
    for i in (1, 3, 2):
        t_copy(i).wait_recv()
    entering = jnp.zeros((32, LANES), F32)
    for n in range(NY - 1):
        entering = jnp.where(n < y, row_decays[n] * entering + t_recv[n], entering)

    def p_copy(i):
        return pltpu.make_async_remote_copy(
            src_ref=p_send.at[lax.rem(z + i, NZ)], dst_ref=i_ref.at[z], send_sem=p_ssem.at[i],
            recv_sem=p_rsem.at[i], device_id={"ctx": z_peer(i)}, device_id_type=MESH,
        )

    for n in range(NZ):
        p_send[n] = (p_ref[n] + reach[n] * entering).astype(BF16)
    for i in FAR_FIRST:
        go(p_copy(i))
    i_ref[z] = p_send[z]

    depth, width = a_ref.shape[2], out_ref.shape[1]
    early, late = slice(0, EARLY), slice(EARLY, length)

    def weight_of(slot):
        return w_ref[pl.ds(pl.multiple_of(slot * depth, depth), depth), :]

    def add(rows, block, slot):
        acc_ref[rows, :] += dot(block, weight_of(slot), ((1,), (0,)))

    def add_inner(slot):
        add(early, al_ref[slot], slot)

    def add_carried(slot):
        parts = []
        for h in range(heads):
            span = slice(h * LANES, (h + 1) * LANES)
            parts.append(
                dot(qt_ref[slot, :, span], g_ref[slot, span, :], ((1,), (0,))).astype(BF16)
            )
        add(early, jnp.concatenate(parts, axis=1), slot)

    def add_late(slot):
        add(late, a_ref[slot], slot)

    q_flow.second()
    acc_ref[...] = jnp.zeros_like(acc_ref)
    need(3)
    q_flow.near(partner)
    al_flow.near(partner)
    add_inner(partner)
    al_flow.first()
    al_flow.second()
    add_inner(left)
    add_inner(right)
    for slot in (left2, right2):
        q_flow.near(slot)
        al_flow.near(slot)
        add_inner(slot)
    q_flow.last()

    for i in FAR_FIRST:
        p_copy(i).wait_recv()
    for h in range(heads):
        span = slice(h * LANES, (h + 1) * LANES)
        state = i_ref[h * 4 : (h + 1) * 4].reshape(LANES, LANES).astype(F32)
        g_ref[tp, span, :] = (state * gain_ref[:, span]).astype(BF16)
    g_flow.own()

    def finish(rows, store):
        squares = None
        for h in range(heads):
            span = slice(h * LANES, (h + 1) * LANES)
            state = i_ref[h * 4 : (h + 1) * 4].reshape(LANES, LANES)
            carried = dot(q_ref[rows, span], state, ((1,), (0,))) * jnp.exp(col_ref[h, rows, :])
            value = att_ref[rows, span] + carried
            squares = value * value if squares is None else squares + value * value
            store(span, (value * gain_ref[:, span]).astype(BF16))
        sq_ref[rows, :] = squares

    def store_late(span, value):
        a_ref[tp, :, span] = value

    def store_own(span, value):
        own_ref[:, span] = value

    finish(late, store_late)
    a_flow.own()
    finish(early, store_own)
    for b in range(tiles):
        rows = slice(b * LANES, (b + 1) * LANES)
        ssq_ref[tp, :, rows] = jnp.sum(jnp.transpose(sq_ref[rows, :]), axis=0, keepdims=True)

    def ssq_copy(n):
        return pltpu.make_async_remote_copy(
            src_ref=ssq_ref.at[tp], dst_ref=ssq_ref.at[tp], send_sem=q_ssem.at[n],
            recv_sem=q_rsem.at[n], device_id={"tp": tp ^ (n + 1)}, device_id_type=MESH,
        )

    def ssq_from(n):
        slot = tp ^ (n + 1)
        return pltpu.make_async_remote_copy(
            src_ref=ssq_ref.at[slot], dst_ref=ssq_ref.at[slot], send_sem=q_ssem.at[n],
            recv_sem=q_rsem.at[n], device_id={"tp": slot}, device_id_type=MESH,
        )

    for n in range(7):
        go(ssq_copy(n))
    add(early, own_ref[...], tp)
    add_late(tp)
    g_flow.near(partner)
    add_carried(partner)
    g_flow.first()
    g_flow.second()
    al_flow.last()
    a_flow.near(partner)
    add_late(partner)
    add_carried(left)
    add_carried(right)
    a_flow.first()
    a_flow.second()
    add_late(left)
    add_late(right)
    g_flow.last()
    add_inner(opposite)
    add_carried(opposite)
    for n in range(7):
        ssq_from(n).wait_recv()
    squares = ssq_ref[0]
    for n in range(1, 8):
        squares = squares + ssq_ref[n]
    scale = lax.rsqrt(squares / (HEADS * HEAD_DIM) + 1e-06)
    for b in range(tiles):
        rows = slice(b * LANES, (b + 1) * LANES)
        sq_ref[rows, :] = column(scale[:, rows])

    def out_copy(rows, n):
        view = pl.ds(rows.start, rows.stop - rows.start)
        return pltpu.make_async_copy(out_ref.at[view], out_hbm.at[view], out_sem.at[n])

    def write(rows, n):
        out_ref[rows, :] = (
            acc_ref[rows, :] * jnp.tile(sq_ref[rows, :], (1, width // LANES))
        ).astype(BF16)
        out_copy(rows, n).start()

    for slot in (left2, right2, opposite2):
        if slot is opposite2:
            q_flow.near(slot)
            al_flow.near(slot)
            add_inner(slot)
        g_flow.near(slot)
        add_carried(slot)
        if slot is not opposite2:
            a_flow.near(slot)
            add_late(slot)
    write(early, 0)
    a_flow.last()
    add_late(opposite)
    a_flow.near(opposite2)
    add_late(opposite2)
    write(late, 1)

    for n in waiting:
        loads[n].wait()
    for copy in sent:
        copy.wait_send()
    out_copy(early, 0).wait()
    out_copy(late, 1).wait()


def per_device(query_rows, key_rows, value_rows, log_decay, norm_gain, out_weight):
    length, features = query_rows.shape
    heads = log_decay.shape[0]
    depth, width = out_weight.shape
    hbm = pl.BlockSpec(memory_space=pltpu.HBM)
    dma = pltpu.SemaphoreType.DMA
    return pl.pallas_call(
        kernel,
        out_shape=jax.ShapeDtypeStruct((length, width), BF16),
        in_specs=[hbm] * 6,
        out_specs=hbm,
        scratch_shapes=[
            pltpu.VMEM((length, width), BF16),
            pltpu.VMEM((heads, length), F32),
            pltpu.VMEM((1, features), F32),
            pltpu.VMEM((length, features), BF16),
            pltpu.VMEM((length, features), BF16),
            pltpu.VMEM((length, features), BF16),
            pltpu.VMEM((depth, width), BF16),
            pltpu.VMEM((16, LANES), F32),
            pltpu.VMEM((heads, length, LANES), F32),
            pltpu.VMEM((length, features), F32),
            pltpu.VMEM((length, width), F32),
            pltpu.VMEM((NZ, 32, LANES), BF16),
            pltpu.VMEM((NZ, 32, LANES), BF16),
            pltpu.VMEM((heads, 1, LANES), F32),
            pltpu.VMEM((NZ, 1, LANES), F32),
            pltpu.VMEM((7, 32, LANES), BF16),
            pltpu.VMEM((7, 1, LANES), F32),
            pltpu.VMEM((NZ, 32, LANES), F32),
            pltpu.VMEM((32, LANES), F32),
            pltpu.VMEM((NY, 32, LANES), F32),
            pltpu.VMEM((1, LANES), F32),
            pltpu.VMEM((NY, 1, LANES), F32),
            pltpu.VMEM((NZ, 32, LANES), BF16),
            pltpu.VMEM((NZ, 32, LANES), BF16),
            pltpu.VMEM((8, EARLY, features), BF16),
            pltpu.VMEM((8, EARLY, features), BF16),
            pltpu.VMEM((8, features, LANES), BF16),
            pltpu.VMEM((8, length - EARLY, features), BF16),
            pltpu.VMEM((EARLY, features), BF16),
            pltpu.VMEM((length, LANES), F32),
            pltpu.VMEM((8, 1, length), F32),
            dma((2,)), dma((6,)),
            dma((NZ,)), dma((NZ,)), dma((NZ,)), dma((NZ,)),
            dma((7,)), dma((7,)), dma((7,)), dma((7,)),
            dma((NY,)), dma((NY,)), dma((NY,)), dma((NY,)),
            dma((NZ,)), dma((NZ,)),
            dma((7,)), dma((7,)),
            dma((4, 14)), dma((4, 8, 2)),
        ],
        compiler_params=pltpu.CompilerParams(
            collective_id=0, has_side_effects=True, vmem_limit_bytes=66650000
        ),
        name="attention_layer",
    )(query_rows, key_rows, value_rows, log_decay, norm_gain.reshape(1, features), out_weight)


def solution(mesh):
    in_specs = (
        P("ctx", "tp"),
        P("ctx", "tp"),
        P("ctx", "tp"),
        P("tp", "ctx"),
        P("tp"),
        P(None, "tp"),
    )
    return jax.shard_map(
        per_device, mesh=mesh, in_specs=in_specs, out_specs=P("ctx", "tp"), check_vma=False
    )
```
